32 devices in a mesh: lat: 8 (over z, y), lev: 4 (over x, core).
Axes of the slice: x: 2, y: 2, z: 4, core: 2. Of those that a mesh axis runs over, the one named last changes fastest.
Arguments:
- field: float32 [4, 320, 4096], P(None, 'lat', 'lev'), may hold values from -6 to 6
- weights: bfloat16 [4, 320, 4096], P(None, 'lat', 'lev'), may hold values from 0 to 0.5
- depart_row: int32 [320, 4096], P('lat', 'lev'), may hold values from -2 to 1
- depart_col: int32 [320, 4096], P('lat', 'lev'), may hold values from -2 to 1
- legendre: bfloat16 [320, 16, 640], P('lat'), may hold values from -6 to 6
- wave_slot: int32 [16], replicated, may hold values from 0 to 15, each once
Outputs:
- updated: float32 [4, 320, 4096], P(None, 'lat', 'lev')
- spectral: float32 [16, 2, 4, 2, 640], P('lat', None, 'lev')
The draws below stay inside these ranges and needn't reach their ends.
Inputs may be any that keep to these rules, and one draw needn't show every extreme that they name: `depart_row`: latitude offsets of departure cells, so that rows i - 2 to i + 2 are read. `depart_col`: longitude offsets of departure cells, so that columns j - 2 to j + 2 are read, periodically. `wave_slot`: A permutation of 0 to 15.
All inputs are finite; a program needn't handle non-finite values.
Results may differ from the reference program's by a relative error of at most 0.0033.
Values may be sent and summed in bfloat16 or wider, within the bound.
A program may use at most 128 MiB of HBM per device.

```python
import math
import jax
import jax.numpy as jnp
from jax import lax

NLON = 4096
NT = 1279
NJ = 640
NLAT = 320
LEV = 4
M_WIN = 16


def place_ends(result, key, low, high):
    index_at = [jax.random.randint(jax.random.fold_in(key, axis), (), 0, length) for axis, length in enumerate(result.shape)]
    main_axis = result.shape.index(max(result.shape))
    next_to = index_at[:main_axis] + [(index_at[main_axis] + 1) % result.shape[main_axis]] + index_at[main_axis + 1:]
    return result.at[tuple(index_at)].set(low).at[tuple(next_to)].set(high)


def shard_levels(rng, dims, split, smallest, top_value):
    def one(axis_at, parts):
        draws = jax.random.uniform(jax.random.fold_in(jax.random.fold_in(rng, 6), axis_at), (parts,), jnp.float32, smallest / len(split), top_value / len(split))
        return jnp.repeat(jnp.exp(draws), dims[axis_at] // parts).reshape((-1,) + (1,) * (len(dims) - axis_at - 1))

    level = one(*split[0])
    for cut in split[1:]:
        level = level * one(*cut)
    return level


def gaussian(rng, shape, spread, reach, split=(), held_as=jnp.bfloat16):
    entries = spread * jax.random.normal(rng, shape, jnp.float32)
    if split:
        entries = entries * shard_levels(rng, shape, split, -0.22, 0.18)
    return jnp.clip(entries, -reach, reach).astype(held_as)


def setup_inputs(seed: int = 0) -> dict:
    streams_of = jax.random.split(jax.random.key(seed), 7)
    field = gaussian(streams_of[0], (LEV, NLAT, NLON), 1.0, 6.0, ((1, 8), (2, 4)), jnp.float32)
    weights = jnp.clip(0.5 * jax.random.uniform(streams_of[1], (4, NLAT, NLON), jnp.float32) ** shard_levels(streams_of[1], (4, NLAT, NLON), ((1, 8), (2, 4)), -0.2, 0.2), 0.0, 0.5).astype(jnp.bfloat16)
    depart_row = place_ends(jax.random.randint(streams_of[2], (NLAT, NLON), -2, 2), jax.random.fold_in(streams_of[2], 1), -2, 1).astype(jnp.int32)
    depart_col = place_ends(jax.random.randint(streams_of[3], (NLAT, NLON), -2, 2), jax.random.fold_in(streams_of[3], 1), -2, 1).astype(jnp.int32)
    legendre = gaussian(streams_of[4], (NLAT, M_WIN, NJ), 1.0, 6.0, ((0, 8),))
    wave_slot = jax.random.permutation(streams_of[5], M_WIN).astype(jnp.int32)
    return {"field": field, "weights": weights, "depart_row": depart_row, "depart_col": depart_col, "legendre": legendre, "wave_slot": wave_slot}


DAMPING = 4.0

def advect(field, weights, depart_row, depart_col):
    padded = jnp.pad(field, ((0, 0), (2, 2), (0, 0)))
    flattened = padded.reshape(LEV, (NLAT + 4) * NLON)
    row_index = jnp.arange(NLAT, dtype=jnp.int32)[:, None] + 2 + depart_row
    col_index = jnp.arange(NLON, dtype=jnp.int32)[None, :] + depart_col
    summed = jnp.zeros((LEV, NLAT * NLON), jnp.float32)
    for row_step in range(2):
        for col_step in range(2):
            source = ((row_index + row_step) * NLON + (col_index + col_step) % NLON).reshape(-1).astype(jnp.int32)
            corner = weights[2 * row_step + col_step].reshape(-1).astype(jnp.float32)
            summed = summed + corner[None, :] * jnp.take(flattened, source, axis=1)
    return summed.reshape(LEV, NLAT, NLON)

def reference(field, weights, depart_row, depart_col, legendre, wave_slot):
    advected = advect(field, weights, depart_row, depart_col)
    wavenumbers = jnp.arange(M_WIN, dtype=jnp.int32) * (NT + 1) // M_WIN
    spectrum = jnp.fft.rfft(advected, axis=2)[:, :, wavenumbers]
    fourier = (jnp.stack([spectrum.real, spectrum.imag], axis=2) / math.sqrt(NLON)).astype(jnp.bfloat16)
    half_lat = NLAT // 2
    north_rows = fourier[:, :half_lat].astype(jnp.float32)
    south_rows = jnp.flip(fourier[:, half_lat:], axis=1).astype(jnp.float32)
    leg_north = legendre[:half_lat].astype(jnp.float32)
    leg_south = jnp.flip(legendre[half_lat:], axis=0).astype(jnp.float32)
    hp = lax.Precision.HIGHEST
    norm_scale = 1.0 / math.sqrt(half_lat)
    even_sums = (jnp.einsum('lkq,vlck->kvcq', leg_north, north_rows, precision=hp) + jnp.einsum('lkq,vlck->kvcq', leg_north, south_rows, precision=hp)) * norm_scale
    odd_sums = (jnp.einsum('lkq,vlck->kvcq', leg_south, north_rows, precision=hp) - jnp.einsum('lkq,vlck->kvcq', leg_south, south_rows, precision=hp)) * norm_scale
    raw_sums = jnp.stack([even_sums, odd_sums], axis=1)
    degree = wavenumbers[:, None, None] + 2 * jnp.arange(NJ, dtype=jnp.int32)[None, None, :] + jnp.arange(2, dtype=jnp.int32)[None, :, None]
    inside = degree <= NT
    factor = 1.0 / (1.0 + DAMPING * (degree * (degree + 1)).astype(jnp.float32) / float(NT * (NT + 1)))
    masked = jnp.where(inside[:, :, None, None, :], raw_sums, jnp.zeros_like(raw_sums))
    damped = masked * factor[:, :, None, None, :]
    change = (damped - masked).astype(jnp.bfloat16).astype(jnp.float32)
    slot_order = jnp.argsort(wave_slot).astype(jnp.int32)
    spectral = jnp.take(damped, slot_order, axis=0)
    inverse_scale = 1.0 / math.sqrt(NJ)
    upper = jnp.einsum('lkq,kvcq->vlck', leg_north, change[:, 0], precision=hp) * inverse_scale
    lower = jnp.einsum('lkq,kvcq->vlck', leg_south, change[:, 1], precision=hp) * inverse_scale
    synthesis = jnp.concatenate([upper + lower, jnp.flip(upper - lower, axis=1)], axis=1)
    real_full = jnp.zeros((LEV, NLAT, NLON // 2 + 1), synthesis.dtype).at[:, :, wavenumbers].set(synthesis[:, :, 0])
    imag_full = jnp.zeros((LEV, NLAT, NLON // 2 + 1), synthesis.dtype).at[:, :, wavenumbers].set(synthesis[:, :, 1])
    increment = jnp.fft.irfft(lax.complex(real_full, imag_full), n=NLON, axis=2) * (NLON / math.sqrt(M_WIN))
    updated = advected + increment
    return (updated, spectral)
```

```python
import functools
import math

import jax
import jax.numpy as jnp
import numpy as np
from jax import lax
from jax.experimental import pallas as pl
from jax.experimental.pallas import tpu as pltpu
from jax.sharding import PartitionSpec as P

NLON = 4096
NT = 1279
DAMPING = 4.0
LANES = 128
HALF = 64
MESH = pl.DeviceIdType.MESH
F32 = jnp.float32
BF16 = jnp.bfloat16


def lon_table(waves):
    m = (np.arange(waves, dtype=np.int64) * (NT + 1)) // waves
    phases = (m[:, None] * np.arange(NLON, dtype=np.int64)[None, :]) % NLON
    angles = phases.astype(np.float64) * (2.0 * math.pi / NLON)
    table = np.concatenate([np.cos(angles), -np.sin(angles)], axis=0) / math.sqrt(NLON)
    table = table.astype(np.float32)
    lead = table.astype(BF16)
    rest = (table - lead.astype(np.float32)).astype(BF16)
    return np.concatenate([lead, rest], axis=0)


def kernel(
    n_lat, n_lev,
    slot_ref, field_hbm, weights_hbm, drow_hbm, dcol_hbm, leg_hbm, table_hbm,
    out_ref, spec_ref,
    ext, shifted, wts, drow, dcol, leg, tab, adv, inv,
    pack_row, pack_col, got_row, got_col, got_corner,
    send_f, got_f, send_x, got_x, sums, send_s, got_s, send_c, got_c,
    chg_slot, chg, send_h, got_h,
    load_sem, halo_send, halo_recv, f_send, f_recv, x_send, x_recv,
    s_send, s_recv, c_send, c_recv, h_send, h_recv,
):
    levels, rows, width = out_ref.shape
    tiles = width // LANES
    waves, steps = leg.shape[1], leg.shape[2]
    l, e = lax.axis_index("lat"), lax.axis_index("lev")
    mirror = n_lat - 1 - l
    has_up, has_down = l > 0, l < n_lat - 1
    east, west = lax.rem(e + 1, n_lev), lax.rem(e + n_lev - 1, n_lev)
    others = lambda start, size: [lax.rem(start + off, size) for off in range(1, size)]

    loads = []

    def load(src, dst):
        copy = pltpu.make_async_copy(src, dst, load_sem.at[len(loads)])
        copy.start()
        loads.append(copy)

    for t in range(tiles):
        load(
            field_hbm.at[:, :, pl.ds(t * LANES, LANES)],
            ext.at[:, t + 1, pl.ds(8, rows), :],
        )
    load(weights_hbm, wts)
    load(drow_hbm, drow)
    load(dcol_hbm, dcol)
    load(table_hbm.at[:, pl.ds(pl.multiple_of(e * width, LANES), width)], tab)
    load(leg_hbm, leg)

    barrier = pltpu.get_barrier_semaphore()

    def greet(lat, lev):
        pl.semaphore_signal(barrier, inc=1, device_id=(lat, lev), device_id_type=MESH)

    for d in others(l, n_lat):
        greet(d, e)
    for d in others(e, n_lev):
        greet(l, d)
        greet(mirror, d)

    @pl.when(has_up)
    def _():
        greet(l - 1, east)
        greet(l - 1, west)

    @pl.when(has_down)
    def _():
        greet(l + 1, east)
        greet(l + 1, west)

    def find(s, carry):
        def step(k, found):
            return jnp.where(slot_ref[k] == s, k, found)

        inv[s] = lax.fori_loop(0, waves, step, jnp.int32(0))
        return carry

    lax.fori_loop(0, waves, find, 0)

    lane = lax.broadcasted_iota(jnp.int32, (rows, LANES), 1)
    for t in range(tiles):
        loads[t].wait()
    for v in range(levels):
        for t in range(tiles):
            cols = slice(t * LANES, (t + 1) * LANES)
            pack_row[0, 2 * v : 2 * v + 2, cols] = ext[v, t + 1, 6 + rows : 8 + rows, :]
            pack_row[1, 2 * v : 2 * v + 2, cols] = ext[v, t + 1, 8:10, :]
    last = jnp.zeros((rows, LANES), F32)
    first = jnp.zeros((rows, LANES), F32)
    for v in range(levels):
        here = (lane == 2 * v) | (lane == 2 * v + 1)
        tail = pltpu.roll(ext[v, tiles, 8 : 8 + rows, :], (2 * v + 2) % LANES, 1)
        last = jnp.where(here, tail, last)
        head = ext[v, 1, 8 : 8 + rows, :]
        if v:
            head = pltpu.roll(head, 2 * v, 1)
        first = jnp.where(here, head, first)
    pack_col[0] = last
    pack_col[1] = first

    n_greet = (n_lat - 1) + 2 * (n_lev - 1)
    n_greet = n_greet + jnp.where(has_up, 2, 0) + jnp.where(has_down, 2, 0)
    pl.semaphore_wait(barrier, n_greet)

    def remote(src, dst, ssem, rsem, lat, lev):
        return pltpu.make_async_remote_copy(
            src_ref=src, dst_ref=dst, send_sem=ssem, recv_sem=rsem,
            device_id=(lat, lev), device_id_type=MESH,
        )

    def halo(n, src, dst, lat, lev):
        return remote(src, dst, halo_send.at[n], halo_recv.at[n], lat, lev)

    bottom, top = pl.ds(rows - 8, 8), pl.ds(0, 8)
    flat = [
        halo(0, pack_col.at[0], got_col.at[0], l, east),
        halo(1, pack_col.at[1], got_col.at[1], l, west),
    ]
    below = [
        halo(2, pack_row.at[0], got_row.at[0], l + 1, e),
        halo(3, pack_col.at[0, bottom], got_corner.at[0], l + 1, east),
        halo(4, pack_col.at[1, bottom], got_corner.at[1], l + 1, west),
    ]
    above = [
        halo(5, pack_row.at[1], got_row.at[1], l - 1, e),
        halo(6, pack_col.at[0, top], got_corner.at[2], l - 1, east),
        halo(7, pack_col.at[1, top], got_corner.at[3], l - 1, west),
    ]

    @pl.when(has_down)
    def _():
        for copy in below:
            copy.start()

    @pl.when(has_up)
    def _():
        for copy in above:
            copy.start()

    for copy in flat:
        copy.start()

    def spread(piece, v):
        return pltpu.roll(piece, LANES - 2 - 2 * v, 1)

    def spread_east(piece, v):
        return pltpu.roll(piece, LANES - 2 * v, 1) if v else piece

    def rim(row0, size, from_west, from_east):
        for v in range(levels):
            ext[v, 0, row0 : row0 + size, :] = spread(from_west, v)
            ext[v, tiles + 1, row0 : row0 + size, :] = spread_east(from_east, v)

    def fill_rows(which, row0):
        for v in range(levels):
            for t in range(tiles):
                cols = slice(t * LANES, (t + 1) * LANES)
                ext[v, t + 1, row0 : row0 + 2, :] = got_row[which, 2 * v : 2 * v + 2, cols]

    @pl.when(has_up)
    def _():
        for copy in below:
            copy.wait_recv()
        fill_rows(0, 6)
        rim(0, 8, got_corner[0], got_corner[1])

    @pl.when(jnp.logical_not(has_up))
    def _():
        ext[:, :, 0:8, :] = jnp.zeros((levels, tiles + 2, 8, LANES), F32)

    @pl.when(has_down)
    def _():
        for copy in above:
            copy.wait_recv()
        fill_rows(1, rows + 8)
        rim(rows + 8, 8, got_corner[2], got_corner[3])

    @pl.when(jnp.logical_not(has_down))
    def _():
        ext[:, :, rows + 8 : rows + 16, :] = jnp.zeros((levels, tiles + 2, 8, LANES), F32)

    for copy in flat:
        copy.wait_recv()
    rim(8, rows, got_col[0], got_col[1])

    tall = rows + 16
    tall_lane = lax.broadcasted_iota(jnp.int32, (tall, LANES), 1)

    def shift_tile(n, carry):
        v, t = n // tiles, n % tiles
        left, here, right = ext[v, t], ext[v, t + 1], ext[v, t + 2]
        for n_move, move in enumerate((-2, -1, 1, 2)):
            amount = (-move) % LANES
            mine = pltpu.roll(here, amount, 1)
            if move < 0:
                moved = jnp.where(tall_lane < -move, pltpu.roll(left, amount, 1), mine)
            else:
                moved = jnp.where(tall_lane >= LANES - move, pltpu.roll(right, amount, 1), mine)
            shifted[n_move, v, t] = moved
        return carry

    lax.fori_loop(0, levels * tiles, shift_tile, 0)

    for n in range(tiles, tiles + 3):
        loads[n].wait()

    def advect_tile(t, carry):
        cols = pl.ds(pl.multiple_of(t * LANES, LANES), LANES)
        corner = [wts[ab, :, cols].astype(F32) for ab in range(4)]
        for g in range(rows // 8):
            band = slice(8 * g, 8 * g + 8)
            dr, dc = drow[band, cols], dcol[band, cols]
            zero = jnp.zeros((8, LANES), F32)
            in_col = {c: dc == c for c in range(-2, 2)}
            in_row = {r: dr == r for r in range(-2, 2)}

            def pick(masks, at, one, two):
                value = zero
                if at - 1 in masks:
                    value = jnp.where(masks[at - 1], two, value)
                if at in masks:
                    value = jnp.where(masks[at], one, value)
                return value

            part = [
                [pick(in_col, c, corner[2 * a][band], corner[2 * a + 1][band]) for c in range(-2, 3)]
                for a in range(2)
            ]
            coef = [
                [pick(in_row, r, part[0][c], part[1][c]) for c in range(5)] for r in range(-2, 3)
            ]
            for v in range(levels):
                total = None
                for r in range(5):
                    at = pl.ds(8 * g + 6 + r, 8)
                    for c in range(5):
                        if c == 2:
                            value = ext[v, t + 1, at, :]
                        else:
                            value = shifted[c if c < 2 else c - 1, v, t, at, :]
                        term = coef[r][c] * value
                        total = term if total is None else total + term
                adv[v * rows + 8 * g : v * rows + 8 * g + 8, cols] = total
        return carry

    lax.fori_loop(0, tiles, advect_tile, 0)

    loads[tiles + 3].wait()
    contract_last = (((1,), (1,)), ((), ()))
    send_f[...] = jnp.zeros_like(send_f)
    for v in range(levels):
        value = adv[v * rows : (v + 1) * rows, :]
        lead = value.astype(BF16)
        rest = (value - lead.astype(F32)).astype(BF16)
        both = lax.dot_general(tab[...], lead, contract_last, preferred_element_type=F32)
        more = lax.dot_general(
            tab[0 : 2 * waves, :], rest, contract_last, preferred_element_type=F32
        )
        coeffs = both[0 : 2 * waves] + both[2 * waves :] + more
        send_f[v, :, 0:rows] = coeffs[0:waves]
        send_f[v, :, HALF : HALF + rows] = coeffs[waves:]
    copies_f = []
    for d in others(e, n_lev):
        copy = remote(send_f.at[d], got_f.at[e], f_send.at[d], f_recv.at[e], l, d)
        copy.start()
        copies_f.append(copy)
    got_f[e] = send_f[e]
    for d in others(e, n_lev):
        remote(send_f.at[d], got_f.at[d], f_send.at[d], f_recv.at[d], l, d).wait_recv()
    total = got_f[0]
    for d in range(1, n_lev):
        total = total + got_f[d]
    fourier = total.astype(BF16)
    send_x[...] = fourier
    copy_x = remote(send_x, got_x, x_send, x_recv, mirror, e)
    copy_x.start()

    at_row = lax.broadcasted_iota(jnp.int32, (LANES, LANES), 0)
    at_col = lax.broadcasted_iota(jnp.int32, (LANES, LANES), 1)
    flip = ((at_row + at_col == rows - 1) & (at_row < HALF) & (at_col < HALF)) | (
        (at_row + at_col == 2 * HALF + rows - 1) & (at_row >= HALF) & (at_col >= HALF)
    )
    flip = flip.astype(F32)
    sign = jnp.where(l < n_lat // 2, 1.0, -1.0).astype(F32)
    loads[tiles + 4].wait()
    copy_x.wait_recv()
    partner = jnp.dot(got_x[...], flip.astype(BF16), preferred_element_type=F32)
    combined = partner + sign * fourier.astype(F32)

    forward_scale = 1.0 / math.sqrt(rows * n_lat // 2)
    group = 16
    for k0 in range(0, waves, group):
        ks = slice(k0, k0 + group)
        real = jnp.zeros((group, steps), F32)
        imag = jnp.zeros((group, steps), F32)
        for i in range(rows):
            values = leg[i, ks, :].astype(F32)
            real = real + values * combined[ks, i : i + 1]
            imag = imag + values * combined[ks, HALF + i : HALF + i + 1]
        sums[0, ks, :] = real * forward_scale
        sums[1, ks, :] = imag * forward_scale
    for s in range(waves):
        k = inv[s]
        send_s[s, 0:1, :] = sums[0, pl.ds(k, 1), :]
        send_s[s, 1:2, :] = sums[1, pl.ds(k, 1), :]
    own = waves // n_lat
    copies_s = []
    for d in others(l, n_lat):
        copy = remote(
            send_s.at[pl.ds(d * own, own)], got_s.at[l], s_send.at[d], s_recv.at[l], d, e
        )
        copy.start()
        copies_s.append(copy)
    got_s[l] = send_s[pl.ds(l * own, own)]
    for d in others(l, n_lat):
        remote(
            send_s.at[pl.ds(d * own, own)], got_s.at[d], s_send.at[d], s_recv.at[d], d, e
        ).wait_recv()

    column = lax.broadcasted_iota(jnp.int32, (2, steps), 1)
    for p in range(2):
        start = p * (n_lat // 2)
        raw = got_s[start]
        for d in range(start + 1, start + n_lat // 2):
            raw = raw + got_s[d]
        for so in range(own):
            wave = inv[l * own + so] * (NT + 1) // waves
            degree = wave + 2 * column + p
            factor = 1.0 / (
                1.0 + DAMPING * (degree * (degree + 1)).astype(F32) / float(NT * (NT + 1))
            )
            masked = jnp.where(degree <= NT, raw[so], 0.0)
            damped = masked * factor
            spec_ref[so, p, 0] = damped
            send_c[p, so] = (damped - masked).astype(BF16)
    copies_c = []
    parity_of = lambda d: d // (n_lat // 2)
    for d in others(l, n_lat):
        copy = remote(send_c.at[parity_of(d)], got_c.at[l], c_send.at[d], c_recv.at[l], d, e)
        copy.start()
        copies_c.append(copy)
    got_c[l] = send_c[parity_of(l)]
    for d in others(l, n_lat):
        remote(
            send_c.at[parity_of(d)], got_c.at[d], c_send.at[d], c_recv.at[d], d, e
        ).wait_recv()

    for d in range(n_lat):
        for so in range(own):
            chg_slot[d * own + so] = got_c[d, so].astype(F32)
    for k in range(waves):
        value = chg_slot[slot_ref[k]]
        chg[0, k : k + 1, :] = value[0:1]
        chg[1, k : k + 1, :] = value[1:2]
    inverse_scale = math.sqrt(NLON) / math.sqrt(waves) / math.sqrt(steps)
    lane = lax.broadcasted_iota(jnp.int32, (group, LANES), 1)
    wave_row = lax.broadcasted_iota(jnp.int32, (group, LANES), 0)
    for k0 in range(0, waves, group):
        ks = slice(k0, k0 + group)
        real, imag = chg[0, ks, :], chg[1, ks, :]
        half = jnp.zeros((group, LANES), F32)
        for i in range(rows):
            values = leg[i, ks, :].astype(F32)
            half = jnp.where(lane == i, jnp.sum(values * real, axis=1, keepdims=True), half)
            half = jnp.where(
                lane == HALF + i, jnp.sum(values * imag, axis=1, keepdims=True), half
            )
        half = half * jnp.where(wave_row + k0 == 0, inverse_scale, 2.0 * inverse_scale)
        send_h[0, ks, :] = half
        send_h[1, ks, :] = jnp.dot(
            half, flip, precision=lax.Precision.HIGHEST, preferred_element_type=F32
        )
    copies_h = []
    for off in range(n_lev):
        d = lax.rem(e + off, n_lev)
        copy = remote(send_h.at[1], got_h.at[1, e], h_send.at[1, d], h_recv.at[1, e], mirror, d)
        copy.start()
        copies_h.append(copy)
    for d in others(e, n_lev):
        copy = remote(send_h.at[0], got_h.at[0, e], h_send.at[0, d], h_recv.at[0, e], l, d)
        copy.start()
        copies_h.append(copy)
    got_h[0, e] = send_h[0]
    for d in others(e, n_lev):
        remote(
            send_h.at[0], got_h.at[0, d], h_send.at[0, d], h_recv.at[0, d], l, d
        ).wait_recv()
    for off in range(n_lev):
        d = lax.rem(e + off, n_lev)
        remote(
            send_h.at[1], got_h.at[1, d], h_send.at[1, d], h_recv.at[1, d], mirror, d
        ).wait_recv()

    stack = []
    for v in range(levels):
        synthesis = got_h[1, v] + sign * got_h[0, v]
        both = jnp.concatenate([synthesis, pltpu.roll(synthesis, HALF, 1)], axis=0)
        stack.append(jnp.transpose(both)[0:rows, :])
    synthesis = jnp.concatenate(stack, axis=0)
    lead = synthesis.astype(BF16)
    rest = (synthesis - lead.astype(F32)).astype(BF16)
    chunk = min(width, 256)
    for j in range(0, width, chunk):
        cols = slice(j, j + chunk)
        table, table_rest = tab[0 : 2 * waves, cols], tab[2 * waves :, cols]
        increment = (
            jnp.dot(lead, table, preferred_element_type=F32)
            + jnp.dot(lead, table_rest, preferred_element_type=F32)
            + jnp.dot(rest, table, preferred_element_type=F32)
        )
        updated = adv[:, cols] + increment
        for v in range(levels):
            out_ref[v, :, cols] = updated[v * rows : (v + 1) * rows]

    for copy in flat + copies_f + [copy_x] + copies_s + copies_c + copies_h:
        copy.wait_send()

    @pl.when(has_down)
    def _():
        for copy in below:
            copy.wait_send()

    @pl.when(has_up)
    def _():
        for copy in above:
            copy.wait_send()


def solution(mesh):
    n_lat, n_lev = mesh.shape["lat"], mesh.shape["lev"]

    def on_device(field, weights, depart_row, depart_col, legendre, wave_slot):
        levels, rows, width = field.shape
        _, waves, steps = legendre.shape
        tiles = width // LANES
        own = waves // n_lat
        table = jnp.asarray(lon_table(waves))
        vmem, dma = pltpu.VMEM, pltpu.SemaphoreType.DMA
        anywhere = pl.BlockSpec(memory_space=pl.ANY)
        in_vmem = pl.BlockSpec(memory_space=pltpu.VMEM)
        return pl.pallas_call(
            functools.partial(kernel, n_lat, n_lev),
            out_shape=(
                jax.ShapeDtypeStruct((levels, rows, width), F32),
                jax.ShapeDtypeStruct((own, 2, 1, 2, steps), F32),
            ),
            in_specs=[pl.BlockSpec(memory_space=pltpu.SMEM)] + [anywhere] * 6,
            out_specs=(in_vmem, in_vmem),
            scratch_shapes=[
                vmem((levels, tiles + 2, rows + 16, LANES), F32),
                vmem((4, levels, tiles, rows + 16, LANES), F32),
                vmem((4, rows, width), BF16),
                vmem((rows, width), jnp.int32),
                vmem((rows, width), jnp.int32),
                vmem((rows, waves, steps), BF16),
                vmem((4 * waves, width), BF16),
                vmem((levels * rows, width), F32),
                pltpu.SMEM((waves,), jnp.int32),
                vmem((2, 2 * levels, width), F32),
                vmem((2, rows, LANES), F32),
                vmem((2, 2 * levels, width), F32),
                vmem((2, rows, LANES), F32),
                vmem((4, 8, LANES), F32),
                vmem((n_lev, waves, LANES), F32),
                vmem((n_lev, waves, LANES), F32),
                vmem((waves, LANES), BF16),
                vmem((waves, LANES), BF16),
                vmem((2, waves, steps), F32),
                vmem((waves, 2, steps), F32),
                vmem((n_lat, own, 2, steps), F32),
                vmem((2, own, 2, steps), BF16),
                vmem((n_lat, own, 2, steps), BF16),
                vmem((waves, 2, steps), F32),
                vmem((2, waves, steps), F32),
                vmem((2, waves, LANES), F32),
                vmem((2, n_lev, waves, LANES), F32),
                dma((tiles + 5,)),
                dma((8,)), dma((8,)),
                dma((n_lev,)), dma((n_lev,)),
                dma, dma,
                dma((n_lat,)), dma((n_lat,)),
                dma((n_lat,)), dma((n_lat,)),
                dma((2, n_lev)), dma((2, n_lev)),
            ],
            compiler_params=pltpu.CompilerParams(
                collective_id=0, has_side_effects=True, vmem_limit_bytes=48 << 20
            ),
        )(wave_slot, field, weights, depart_row, depart_col, legendre, table)

    placed = (
        P(None, "lat", "lev"),
        P(None, "lat", "lev"),
        P("lat", "lev"),
        P("lat", "lev"),
        P("lat", None, None),
        P(),
    )
    return jax.shard_map(
        on_device,
        mesh=mesh,
        in_specs=placed,
        out_specs=(P(None, "lat", "lev"), P("lat", None, "lev", None, None)),
        check_vma=False,
    )
```

```python
import functools
import math

import jax
import jax.numpy as jnp
import numpy as np
from jax import lax
from jax.experimental import pallas as pl
from jax.experimental.pallas import tpu as pltpu
from jax.sharding import PartitionSpec as P

NLON = 4096
NT = 1279
DAMPING = 4.0
LANES = 128
HALF = 64
MESH = pl.DeviceIdType.MESH
F32 = jnp.float32
BF16 = jnp.bfloat16


def lon_table(waves):
    m = (np.arange(waves, dtype=np.int64) * (NT + 1)) // waves
    phases = (m[:, None] * np.arange(NLON, dtype=np.int64)[None, :]) % NLON
    angles = phases.astype(np.float64) * (2.0 * math.pi / NLON)
    table = np.concatenate([np.cos(angles), -np.sin(angles)], axis=0) / math.sqrt(NLON)
    table = table.astype(np.float32)
    lead = table.astype(BF16)
    rest = (table - lead.astype(np.float32)).astype(BF16)
    return np.concatenate([lead, rest], axis=0)


def kernel(
    n_lat, n_lev,
    slot_ref, field_hbm, weights_hbm, drow_hbm, dcol_hbm, leg_hbm, table_hbm,
    out_ref, spec_ref,
    ext, shifted, wts, drow, dcol, leg, tab, adv, inv,
    pack_row, pack_col, got_row, got_col, got_corner,
    send_f, got_f, send_x, got_x, sums, send_s, got_s, send_c, got_c,
    chg_slot, chg, send_h, got_h,
    load_sem, halo_send, halo_recv, f_send, f_recv, x_send, x_recv,
    s_send, s_recv, c_send, c_recv, h_send, h_recv,
):
    levels, rows, width = out_ref.shape
    tiles = width // LANES
    waves, steps = leg.shape[1], leg.shape[2]
    l, e = lax.axis_index("lat"), lax.axis_index("lev")
    mirror = n_lat - 1 - l
    has_up, has_down = l > 0, l < n_lat - 1
    east, west = lax.rem(e + 1, n_lev), lax.rem(e + n_lev - 1, n_lev)
    others = lambda start, size: [lax.rem(start + off, size) for off in range(1, size)]

    loads = []

    def load(src, dst):
        copy = pltpu.make_async_copy(src, dst, load_sem.at[len(loads)])
        copy.start()
        loads.append(copy)

    for t in range(tiles):
        load(
            field_hbm.at[:, :, pl.ds(t * LANES, LANES)],
            ext.at[:, t + 1, pl.ds(8, rows), :],
        )
    load(weights_hbm, wts)
    load(drow_hbm, drow)
    load(dcol_hbm, dcol)
    load(table_hbm.at[:, pl.ds(pl.multiple_of(e * width, LANES), width)], tab)
    load(leg_hbm, leg)

    barrier = pltpu.get_barrier_semaphore()

    def greet(lat, lev):
        pl.semaphore_signal(barrier, inc=1, device_id=(lat, lev), device_id_type=MESH)

    for d in others(l, n_lat):
        greet(d, e)
    for d in others(e, n_lev):
        greet(l, d)
        greet(mirror, d)

    @pl.when(has_up)
    def _():
        greet(l - 1, east)
        greet(l - 1, west)

    @pl.when(has_down)
    def _():
        greet(l + 1, east)
        greet(l + 1, west)

    def find(s, carry):
        def step(k, found):
            return jnp.where(slot_ref[k] == s, k, found)

        inv[s] = lax.fori_loop(0, waves, step, jnp.int32(0))
        return carry

    lax.fori_loop(0, waves, find, 0)

    lane = lax.broadcasted_iota(jnp.int32, (rows, LANES), 1)
    for t in range(tiles):
        loads[t].wait()
    for v in range(levels):
        for t in range(tiles):
            cols = slice(t * LANES, (t + 1) * LANES)
            pack_row[0, 2 * v : 2 * v + 2, cols] = ext[v, t + 1, 6 + rows : 8 + rows, :]
            pack_row[1, 2 * v : 2 * v + 2, cols] = ext[v, t + 1, 8:10, :]
    last = jnp.zeros((rows, LANES), F32)
    first = jnp.zeros((rows, LANES), F32)
    for v in range(levels):
        here = (lane == 2 * v) | (lane == 2 * v + 1)
        tail = pltpu.roll(ext[v, tiles, 8 : 8 + rows, :], (2 * v + 2) % LANES, 1)
        last = jnp.where(here, tail, last)
        head = ext[v, 1, 8 : 8 + rows, :]
        if v:
            head = pltpu.roll(head, 2 * v, 1)
        first = jnp.where(here, head, first)
    pack_col[0] = last
    pack_col[1] = first

    def shift_block(v, t, row0, size):
        at = pl.ds(row0, size)
        at_lane = lax.broadcasted_iota(jnp.int32, (size, LANES), 1)
        left, here, right = ext[v, t, at, :], ext[v, t + 1, at, :], ext[v, t + 2, at, :]
        for n_move, move in enumerate((-2, -1, 1, 2)):
            amount = (-move) % LANES
            mine = pltpu.roll(here, amount, 1)
            if move < 0:
                moved = jnp.where(at_lane < -move, pltpu.roll(left, amount, 1), mine)
            else:
                moved = jnp.where(at_lane >= LANES - move, pltpu.roll(right, amount, 1), mine)
            shifted[n_move, v, t, at, :] = moved

    def shift_inner(chosen):
        def step(t, carry):
            for v in chosen:
                shift_block(v, t, 8, rows)
            return carry

        lax.fori_loop(1, tiles - 1, step, 0)

    groups = rows // 8

    def advect(t, chosen):
        cols = pl.ds(pl.multiple_of(t * LANES, LANES), LANES)
        corner = [wts[ab, :, cols].astype(F32) for ab in range(4)]
        for g in chosen:
            band = slice(8 * g, 8 * g + 8)
            dr, dc = drow[band, cols], dcol[band, cols]
            zero = jnp.zeros((8, LANES), F32)
            in_col = {c: dc == c for c in range(-2, 2)}
            in_row = {r: dr == r for r in range(-2, 2)}

            def pick(masks, at, one, two):
                value = zero
                if at - 1 in masks:
                    value = jnp.where(masks[at - 1], two, value)
                if at in masks:
                    value = jnp.where(masks[at], one, value)
                return value

            part = [
                [pick(in_col, c, corner[2 * a][band], corner[2 * a + 1][band]) for c in range(-2, 3)]
                for a in range(2)
            ]
            coef = [
                [pick(in_row, r, part[0][c], part[1][c]) for c in range(5)] for r in range(-2, 3)
            ]
            for v in range(levels):
                total = None
                for r in range(5):
                    at = pl.ds(8 * g + 6 + r, 8)
                    for c in range(5):
                        if c == 2:
                            value = ext[v, t + 1, at, :]
                        else:
                            value = shifted[c if c < 2 else c - 1, v, t, at, :]
                        term = coef[r][c] * value
                        total = term if total is None else total + term
                adv[v * rows + 8 * g : v * rows + 8 * g + 8, cols] = total

    def advect_inner(t, carry):
        advect(t, range(1, groups - 1))
        return carry

    shift_inner(range(levels // 2))

    n_greet = (n_lat - 1) + 2 * (n_lev - 1)
    n_greet = n_greet + jnp.where(has_up, 2, 0) + jnp.where(has_down, 2, 0)
    pl.semaphore_wait(barrier, n_greet)

    def remote(src, dst, ssem, rsem, lat, lev):
        return pltpu.make_async_remote_copy(
            src_ref=src, dst_ref=dst, send_sem=ssem, recv_sem=rsem,
            device_id=(lat, lev), device_id_type=MESH,
        )

    def halo(n, src, dst, lat, lev):
        return remote(src, dst, halo_send.at[n], halo_recv.at[n], lat, lev)

    bottom, top = pl.ds(rows - 8, 8), pl.ds(0, 8)
    flat = [
        halo(0, pack_col.at[0], got_col.at[0], l, east),
        halo(1, pack_col.at[1], got_col.at[1], l, west),
    ]
    below = [
        halo(2, pack_row.at[0], got_row.at[0], l + 1, e),
        halo(3, pack_col.at[0, bottom], got_corner.at[0], l + 1, east),
        halo(4, pack_col.at[1, bottom], got_corner.at[1], l + 1, west),
    ]
    above = [
        halo(5, pack_row.at[1], got_row.at[1], l - 1, e),
        halo(6, pack_col.at[0, top], got_corner.at[2], l - 1, east),
        halo(7, pack_col.at[1, top], got_corner.at[3], l - 1, west),
    ]

    @pl.when(has_down)
    def _():
        for copy in below:
            copy.start()

    @pl.when(has_up)
    def _():
        for copy in above:
            copy.start()

    for copy in flat:
        copy.start()

    shift_inner(range(levels // 2, levels))
    for n in range(tiles, tiles + 3):
        loads[n].wait()
    lax.fori_loop(1, tiles - 1, advect_inner, 0)

    def spread(piece, v):
        return pltpu.roll(piece, LANES - 2 - 2 * v, 1)

    def spread_east(piece, v):
        return pltpu.roll(piece, LANES - 2 * v, 1) if v else piece

    def rim(row0, size, from_west, from_east):
        for v in range(levels):
            ext[v, 0, row0 : row0 + size, :] = spread(from_west, v)
            ext[v, tiles + 1, row0 : row0 + size, :] = spread_east(from_east, v)

    def fill_rows(which, row0):
        for v in range(levels):
            for t in range(tiles):
                cols = slice(t * LANES, (t + 1) * LANES)
                ext[v, t + 1, row0 : row0 + 2, :] = got_row[which, 2 * v : 2 * v + 2, cols]

    @pl.when(has_up)
    def _():
        for copy in below:
            copy.wait_recv()
        fill_rows(0, 6)
        rim(0, 8, got_corner[0], got_corner[1])

    @pl.when(jnp.logical_not(has_up))
    def _():
        ext[:, :, 0:8, :] = jnp.zeros((levels, tiles + 2, 8, LANES), F32)

    @pl.when(has_down)
    def _():
        for copy in above:
            copy.wait_recv()
        fill_rows(1, rows + 8)
        rim(rows + 8, 8, got_corner[2], got_corner[3])

    @pl.when(jnp.logical_not(has_down))
    def _():
        ext[:, :, rows + 8 : rows + 16, :] = jnp.zeros((levels, tiles + 2, 8, LANES), F32)

    for copy in flat:
        copy.wait_recv()
    rim(8, rows, got_col[0], got_col[1])

    def shift_rims(t, carry):
        for v in range(levels):
            shift_block(v, t, 0, 8)
            shift_block(v, t, rows + 8, 8)
        return carry

    def shift_edge(n, carry):
        for v in range(levels):
            shift_block(v, n * (tiles - 1), 8, rows)
        return carry

    edges = min(tiles, 2)
    lax.fori_loop(0, edges, shift_edge, 0)
    lax.fori_loop(0, tiles, shift_rims, 0)
    outer = sorted({0, groups - 1})

    def advect_rims(t, carry):
        advect(t, outer)
        return carry

    def advect_edge(n, carry):
        advect(n * (tiles - 1), range(groups))
        return carry

    lax.fori_loop(0, edges, advect_edge, 0)
    lax.fori_loop(1, tiles - 1, advect_rims, 0)

    loads[tiles + 3].wait()
    contract_last = (((1,), (1,)), ((), ()))
    send_f[...] = jnp.zeros_like(send_f)
    for v in range(levels):
        value = adv[v * rows : (v + 1) * rows, :]
        lead = value.astype(BF16)
        rest = (value - lead.astype(F32)).astype(BF16)
        both = lax.dot_general(tab[...], lead, contract_last, preferred_element_type=F32)
        more = lax.dot_general(
            tab[0 : 2 * waves, :], rest, contract_last, preferred_element_type=F32
        )
        coeffs = both[0 : 2 * waves] + both[2 * waves :] + more
        send_f[v, :, 0:rows] = coeffs[0:waves]
        send_f[v, :, HALF : HALF + rows] = coeffs[waves:]
    copies_f = []
    for d in others(e, n_lev):
        copy = remote(send_f.at[d], got_f.at[e], f_send.at[d], f_recv.at[e], l, d)
        copy.start()
        copies_f.append(copy)
    got_f[e] = send_f[e]
    for d in others(e, n_lev):
        remote(send_f.at[d], got_f.at[d], f_send.at[d], f_recv.at[d], l, d).wait_recv()
    total = got_f[0]
    for d in range(1, n_lev):
        total = total + got_f[d]
    fourier = total.astype(BF16)
    send_x[...] = fourier
    copy_x = remote(send_x, got_x, x_send, x_recv, mirror, e)
    copy_x.start()

    at_row = lax.broadcasted_iota(jnp.int32, (LANES, LANES), 0)
    at_col = lax.broadcasted_iota(jnp.int32, (LANES, LANES), 1)
    flip = ((at_row + at_col == rows - 1) & (at_row < HALF) & (at_col < HALF)) | (
        (at_row + at_col == 2 * HALF + rows - 1) & (at_row >= HALF) & (at_col >= HALF)
    )
    flip = flip.astype(F32)
    sign = jnp.where(l < n_lat // 2, 1.0, -1.0).astype(F32)
    loads[tiles + 4].wait()
    copy_x.wait_recv()
    partner = jnp.dot(got_x[...], flip.astype(BF16), preferred_element_type=F32)
    combined = partner + sign * fourier.astype(F32)

    forward_scale = 1.0 / math.sqrt(rows * n_lat // 2)
    group = 16
    for k0 in range(0, waves, group):
        ks = slice(k0, k0 + group)
        real = jnp.zeros((group, steps), F32)
        imag = jnp.zeros((group, steps), F32)
        for i in range(rows):
            values = leg[i, ks, :].astype(F32)
            real = real + values * combined[ks, i : i + 1]
            imag = imag + values * combined[ks, HALF + i : HALF + i + 1]
        sums[0, ks, :] = real * forward_scale
        sums[1, ks, :] = imag * forward_scale
    for s in range(waves):
        k = inv[s]
        chg_slot[s, 0:1, :] = sums[0, pl.ds(k, 1), :]
        chg_slot[s, 1:2, :] = sums[1, pl.ds(k, 1), :]
    send_s[...] = chg_slot[...].astype(BF16)
    own = waves // n_lat
    copies_s = []
    for d in others(l, n_lat):
        copy = remote(
            send_s.at[pl.ds(d * own, own)], got_s.at[l], s_send.at[d], s_recv.at[l], d, e
        )
        copy.start()
        copies_s.append(copy)
    got_s[l] = send_s[pl.ds(l * own, own)]
    for d in others(l, n_lat):
        remote(
            send_s.at[pl.ds(d * own, own)], got_s.at[d], s_send.at[d], s_recv.at[d], d, e
        ).wait_recv()

    column = lax.broadcasted_iota(jnp.int32, (2, steps), 1)
    for p in range(2):
        start = p * (n_lat // 2)
        raw = got_s[start].astype(F32)
        for d in range(start + 1, start + n_lat // 2):
            raw = raw + got_s[d].astype(F32)
        for so in range(own):
            wave = inv[l * own + so] * (NT + 1) // waves
            degree = wave + 2 * column + p
            factor = 1.0 / (
                1.0 + DAMPING * (degree * (degree + 1)).astype(F32) / float(NT * (NT + 1))
            )
            masked = jnp.where(degree <= NT, raw[so], 0.0)
            damped = masked * factor
            spec_ref[so, p, 0] = damped
            send_c[p, so] = (damped - masked).astype(BF16)
    copies_c = []
    parity_of = lambda d: d // (n_lat // 2)
    for d in others(l, n_lat):
        copy = remote(send_c.at[parity_of(d)], got_c.at[l], c_send.at[d], c_recv.at[l], d, e)
        copy.start()
        copies_c.append(copy)
    got_c[l] = send_c[parity_of(l)]
    for d in others(l, n_lat):
        remote(
            send_c.at[parity_of(d)], got_c.at[d], c_send.at[d], c_recv.at[d], d, e
        ).wait_recv()

    for d in range(n_lat):
        for so in range(own):
            chg_slot[d * own + so] = got_c[d, so].astype(F32)
    for k in range(waves):
        value = chg_slot[slot_ref[k]]
        chg[0, k : k + 1, :] = value[0:1]
        chg[1, k : k + 1, :] = value[1:2]
    inverse_scale = math.sqrt(NLON) / math.sqrt(waves) / math.sqrt(steps)
    lane = lax.broadcasted_iota(jnp.int32, (group, LANES), 1)
    wave_row = lax.broadcasted_iota(jnp.int32, (group, LANES), 0)
    for k0 in range(0, waves, group):
        ks = slice(k0, k0 + group)
        real, imag = chg[0, ks, :], chg[1, ks, :]
        half = jnp.zeros((group, LANES), F32)
        for i in range(rows):
            values = leg[i, ks, :].astype(F32)
            half = jnp.where(lane == i, jnp.sum(values * real, axis=1, keepdims=True), half)
            half = jnp.where(
                lane == HALF + i, jnp.sum(values * imag, axis=1, keepdims=True), half
            )
        half = half * jnp.where(wave_row + k0 == 0, inverse_scale, 2.0 * inverse_scale)
        send_h[0, ks, :] = half
        send_h[1, ks, :] = jnp.dot(
            half, flip, precision=lax.Precision.HIGHEST, preferred_element_type=F32
        )
    copies_h = []
    for off in range(n_lev):
        d = lax.rem(e + off, n_lev)
        copy = remote(send_h.at[1], got_h.at[1, e], h_send.at[1, d], h_recv.at[1, e], mirror, d)
        copy.start()
        copies_h.append(copy)
    for d in others(e, n_lev):
        copy = remote(send_h.at[0], got_h.at[0, e], h_send.at[0, d], h_recv.at[0, e], l, d)
        copy.start()
        copies_h.append(copy)
    got_h[0, e] = send_h[0]
    for d in others(e, n_lev):
        remote(
            send_h.at[0], got_h.at[0, d], h_send.at[0, d], h_recv.at[0, d], l, d
        ).wait_recv()
    for off in range(n_lev):
        d = lax.rem(e + off, n_lev)
        remote(
            send_h.at[1], got_h.at[1, d], h_send.at[1, d], h_recv.at[1, d], mirror, d
        ).wait_recv()

    stack = []
    for v in range(levels):
        synthesis = got_h[1, v] + sign * got_h[0, v]
        both = jnp.concatenate([synthesis, pltpu.roll(synthesis, HALF, 1)], axis=0)
        stack.append(jnp.transpose(both)[0:rows, :])
    synthesis = jnp.concatenate(stack, axis=0)
    lead = synthesis.astype(BF16)
    rest = (synthesis - lead.astype(F32)).astype(BF16)
    chunk = min(width, 256)
    for j in range(0, width, chunk):
        cols = slice(j, j + chunk)
        table, table_rest = tab[0 : 2 * waves, cols], tab[2 * waves :, cols]
        increment = (
            jnp.dot(lead, table, preferred_element_type=F32)
            + jnp.dot(lead, table_rest, preferred_element_type=F32)
            + jnp.dot(rest, table, preferred_element_type=F32)
        )
        updated = adv[:, cols] + increment
        for v in range(levels):
            out_ref[v, :, cols] = updated[v * rows : (v + 1) * rows]

    for copy in flat + copies_f + [copy_x] + copies_s + copies_c + copies_h:
        copy.wait_send()

    @pl.when(has_down)
    def _():
        for copy in below:
            copy.wait_send()

    @pl.when(has_up)
    def _():
        for copy in above:
            copy.wait_send()


def solution(mesh):
    n_lat, n_lev = mesh.shape["lat"], mesh.shape["lev"]

    def on_device(field, weights, depart_row, depart_col, legendre, wave_slot):
        levels, rows, width = field.shape
        _, waves, steps = legendre.shape
        tiles = width // LANES
        own = waves // n_lat
        table = jnp.asarray(lon_table(waves))
        vmem, dma = pltpu.VMEM, pltpu.SemaphoreType.DMA
        anywhere = pl.BlockSpec(memory_space=pltpu.HBM)
        in_vmem = pl.BlockSpec(memory_space=pltpu.VMEM)
        return pl.pallas_call(
            functools.partial(kernel, n_lat, n_lev),
            out_shape=(
                jax.ShapeDtypeStruct((levels, rows, width), F32),
                jax.ShapeDtypeStruct((own, 2, 1, 2, steps), F32),
            ),
            in_specs=[pl.BlockSpec(memory_space=pltpu.SMEM)] + [anywhere] * 6,
            out_specs=(in_vmem, in_vmem),
            scratch_shapes=[
                vmem((levels, tiles + 2, rows + 16, LANES), F32),
                vmem((4, levels, tiles, rows + 16, LANES), F32),
                vmem((4, rows, width), BF16),
                vmem((rows, width), jnp.int32),
                vmem((rows, width), jnp.int32),
                vmem((rows, waves, steps), BF16),
                vmem((4 * waves, width), BF16),
                vmem((levels * rows, width), F32),
                pltpu.SMEM((waves,), jnp.int32),
                vmem((2, 2 * levels, width), F32),
                vmem((2, rows, LANES), F32),
                vmem((2, 2 * levels, width), F32),
                vmem((2, rows, LANES), F32),
                vmem((4, 8, LANES), F32),
                vmem((n_lev, waves, LANES), F32),
                vmem((n_lev, waves, LANES), F32),
                vmem((waves, LANES), BF16),
                vmem((waves, LANES), BF16),
                vmem((2, waves, steps), F32),
                vmem((waves, 2, steps), BF16),
                vmem((n_lat, own, 2, steps), BF16),
                vmem((2, own, 2, steps), BF16),
                vmem((n_lat, own, 2, steps), BF16),
                vmem((waves, 2, steps), F32),
                vmem((2, waves, steps), F32),
                vmem((2, waves, LANES), F32),
                vmem((2, n_lev, waves, LANES), F32),
                dma((tiles + 5,)),
                dma((8,)), dma((8,)),
                dma((n_lev,)), dma((n_lev,)),
                dma, dma,
                dma((n_lat,)), dma((n_lat,)),
                dma((n_lat,)), dma((n_lat,)),
                dma((2, n_lev)), dma((2, n_lev)),
            ],
            compiler_params=pltpu.CompilerParams(
                collective_id=0, has_side_effects=True, vmem_limit_bytes=63 << 20
            ),
        )(wave_slot, field, weights, depart_row, depart_col, legendre, table)

    placed = (
        P(None, "lat", "lev"),
        P(None, "lat", "lev"),
        P("lat", "lev"),
        P("lat", "lev"),
        P("lat", None, None),
        P(),
    )
    return jax.shard_map(
        on_device,
        mesh=mesh,
        in_specs=placed,
        out_specs=(P(None, "lat", "lev"), P("lat", None, "lev", None, None)),
        check_vma=False,
    )
```

```python
import functools
import math

import jax
import jax.numpy as jnp
import numpy as np
from jax import lax
from jax.experimental import pallas as pl
from jax.experimental.pallas import tpu as pltpu
from jax.sharding import PartitionSpec as P

NLON = 4096
NT = 1279
DAMPING = 4.0
LANES = 128
HALF = 64
MESH = pl.DeviceIdType.MESH
F32 = jnp.float32
BF16 = jnp.bfloat16


def lon_table(waves):
    m = (np.arange(waves, dtype=np.int64) * (NT + 1)) // waves
    phases = (m[:, None] * np.arange(NLON, dtype=np.int64)[None, :]) % NLON
    angles = phases.astype(np.float64) * (2.0 * math.pi / NLON)
    table = np.concatenate([np.cos(angles), -np.sin(angles)], axis=0) / math.sqrt(NLON)
    table = table.astype(np.float32)
    lead = table.astype(BF16)
    rest = (table - lead.astype(np.float32)).astype(BF16)
    return np.concatenate([lead, rest], axis=0)


def kernel(
    n_lat, n_lev,
    slot_ref, field_hbm, weights_hbm, drow_hbm, dcol_hbm, leg_hbm, table_hbm,
    out_ref, spec_ref,
    ext, shifted, wts, drow, dcol, leg, tab, adv, inv,
    pack_row, pack_col, got_row, got_col, got_corner,
    send_f, got_f, send_x, got_x, sums, send_s, got_s, send_c, got_c,
    chg_slot, chg, send_h, got_h,
    load_sem, halo_send, halo_recv, f_send, f_recv, x_send, x_recv,
    s_send, s_recv, c_send, c_recv, h_send, h_recv,
):
    levels, rows, width = out_ref.shape
    tiles = width // LANES
    waves, steps = leg.shape[1], leg.shape[2]
    l, e = lax.axis_index("lat"), lax.axis_index("lev")
    mirror = n_lat - 1 - l
    has_up, has_down = l > 0, l < n_lat - 1
    east, west = lax.rem(e + 1, n_lev), lax.rem(e + n_lev - 1, n_lev)
    others = lambda start, size: [lax.rem(start + off, size) for off in range(1, size)]

    loads = []

    def load(src, dst):
        copy = pltpu.make_async_copy(src, dst, load_sem.at[len(loads)])
        copy.start()
        loads.append(copy)

    for t in range(tiles):
        load(
            field_hbm.at[:, :, pl.ds(t * LANES, LANES)],
            ext.at[:, t + 1, pl.ds(8, rows), :],
        )
    load(weights_hbm, wts)
    load(drow_hbm, drow)
    load(dcol_hbm, dcol)
    load(table_hbm.at[:, pl.ds(pl.multiple_of(e * width, LANES), width)], tab)
    load(leg_hbm, leg)

    barrier = pltpu.get_barrier_semaphore()

    def greet(lat, lev):
        pl.semaphore_signal(barrier, inc=1, device_id=(lat, lev), device_id_type=MESH)

    for d in others(l, n_lat):
        greet(d, e)
    for d in others(e, n_lev):
        greet(l, d)
        greet(mirror, d)

    @pl.when(has_up)
    def _():
        greet(l - 1, east)
        greet(l - 1, west)

    @pl.when(has_down)
    def _():
        greet(l + 1, east)
        greet(l + 1, west)

    lane = lax.broadcasted_iota(jnp.int32, (rows, LANES), 1)
    for t in range(tiles):
        loads[t].wait()
    for v in range(levels):
        for t in range(tiles):
            cols = slice(t * LANES, (t + 1) * LANES)
            pack_row[0, 2 * v : 2 * v + 2, cols] = ext[v, t + 1, 6 + rows : 8 + rows, :]
            pack_row[1, 2 * v : 2 * v + 2, cols] = ext[v, t + 1, 8:10, :]
    last = jnp.zeros((rows, LANES), F32)
    first = jnp.zeros((rows, LANES), F32)
    for v in range(levels):
        here = (lane == 2 * v) | (lane == 2 * v + 1)
        tail = pltpu.roll(ext[v, tiles, 8 : 8 + rows, :], (2 * v + 2) % LANES, 1)
        last = jnp.where(here, tail, last)
        head = ext[v, 1, 8 : 8 + rows, :]
        if v:
            head = pltpu.roll(head, 2 * v, 1)
        first = jnp.where(here, head, first)
    pack_col[0] = last
    pack_col[1] = first

    def shift_block(v, t, row0, size, moves=(-2, -1, 1, 2)):
        at = pl.ds(row0, size)
        at_lane = lax.broadcasted_iota(jnp.int32, (size, LANES), 1)
        here = ext[v, t + 1, at, :]
        left = ext[v, t, at, :] if min(moves) < 0 else None
        right = ext[v, t + 2, at, :] if max(moves) > 0 else None
        for move in moves:
            n_move = (-2, -1, 1, 2).index(move)
            amount = (-move) % LANES
            mine = pltpu.roll(here, amount, 1)
            if move < 0:
                moved = jnp.where(at_lane < -move, pltpu.roll(left, amount, 1), mine)
            else:
                moved = jnp.where(at_lane >= LANES - move, pltpu.roll(right, amount, 1), mine)
            shifted[n_move, v, t, at, :] = moved

    def shift_inner(chosen):
        def step(t, carry):
            for v in chosen:
                shift_block(v, t, 8, rows)
            return carry

        lax.fori_loop(1, tiles - 1, step, 0)

    groups = rows // 8

    def advect(t, chosen):
        cols = pl.ds(pl.multiple_of(t * LANES, LANES), LANES)
        corner = [wts[ab, :, cols].astype(F32) for ab in range(4)]
        for g in chosen:
            band = slice(8 * g, 8 * g + 8)
            dr, dc = drow[band, cols], dcol[band, cols]
            zero = jnp.zeros((8, LANES), F32)
            in_col = {c: dc == c for c in range(-2, 2)}
            in_row = {r: dr == r for r in range(-2, 2)}

            def pick(masks, at, one, two):
                value = zero
                if at - 1 in masks:
                    value = jnp.where(masks[at - 1], two, value)
                if at in masks:
                    value = jnp.where(masks[at], one, value)
                return value

            part = [
                [pick(in_col, c, corner[2 * a][band], corner[2 * a + 1][band]) for c in range(-2, 3)]
                for a in range(2)
            ]
            coef = [
                [pick(in_row, r, part[0][c], part[1][c]) for c in range(5)] for r in range(-2, 3)
            ]
            for v in range(levels):
                total = None
                for r in range(5):
                    at = pl.ds(8 * g + 6 + r, 8)
                    for c in range(5):
                        if c == 2:
                            value = ext[v, t + 1, at, :]
                        else:
                            value = shifted[c if c < 2 else c - 1, v, t, at, :]
                        term = coef[r][c] * value
                        total = term if total is None else total + term
                adv[v * rows + 8 * g : v * rows + 8 * g + 8, cols] = total

    def advect_inner(t, carry):
        advect(t, range(1, groups - 1))
        return carry

    shift_inner(range(levels // 2))

    n_greet = (n_lat - 1) + 2 * (n_lev - 1)
    n_greet = n_greet + jnp.where(has_up, 2, 0) + jnp.where(has_down, 2, 0)
    pl.semaphore_wait(barrier, n_greet)

    def remote(src, dst, ssem, rsem, lat, lev):
        return pltpu.make_async_remote_copy(
            src_ref=src, dst_ref=dst, send_sem=ssem, recv_sem=rsem,
            device_id=(lat, lev), device_id_type=MESH,
        )

    def halo(n, src, dst, lat, lev):
        return remote(src, dst, halo_send.at[n], halo_recv.at[n], lat, lev)

    bottom, top = pl.ds(rows - 8, 8), pl.ds(0, 8)
    flat = [
        halo(0, pack_col.at[0], got_col.at[0], l, east),
        halo(1, pack_col.at[1], got_col.at[1], l, west),
    ]
    below = [
        halo(2, pack_row.at[0], got_row.at[0], l + 1, e),
        halo(3, pack_col.at[0, bottom], got_corner.at[0], l + 1, east),
        halo(4, pack_col.at[1, bottom], got_corner.at[1], l + 1, west),
    ]
    above = [
        halo(5, pack_row.at[1], got_row.at[1], l - 1, e),
        halo(6, pack_col.at[0, top], got_corner.at[2], l - 1, east),
        halo(7, pack_col.at[1, top], got_corner.at[3], l - 1, west),
    ]

    @pl.when(has_down)
    def _():
        for copy in below:
            copy.start()

    @pl.when(has_up)
    def _():
        for copy in above:
            copy.start()

    for copy in flat:
        copy.start()

    def find(s, carry):
        def step(k, found):
            return jnp.where(slot_ref[k] == s, k, found)

        inv[s] = lax.fori_loop(0, waves, step, jnp.int32(0))
        return carry

    lax.fori_loop(0, waves, find, 0)

    shift_inner(range(levels // 2, levels))
    if tiles > 1:
        for v in range(levels):
            shift_block(v, 0, 8, rows, (1, 2))
            shift_block(v, tiles - 1, 8, rows, (-2, -1))
    for n in range(tiles, tiles + 3):
        loads[n].wait()
    lax.fori_loop(1, tiles - 1, advect_inner, 0)

    def spread(piece, v):
        return pltpu.roll(piece, LANES - 2 - 2 * v, 1)

    def spread_east(piece, v):
        return pltpu.roll(piece, LANES - 2 * v, 1) if v else piece

    def rim(row0, size, from_west, from_east):
        for v in range(levels):
            ext[v, 0, row0 : row0 + size, :] = spread(from_west, v)
            ext[v, tiles + 1, row0 : row0 + size, :] = spread_east(from_east, v)

    def fill_rows(which, row0):
        for v in range(levels):
            for t in range(tiles):
                cols = slice(t * LANES, (t + 1) * LANES)
                ext[v, t + 1, row0 : row0 + 2, :] = got_row[which, 2 * v : 2 * v + 2, cols]

    @pl.when(has_up)
    def _():
        for copy in below:
            copy.wait_recv()
        fill_rows(0, 6)
        rim(0, 8, got_corner[0], got_corner[1])

    @pl.when(jnp.logical_not(has_up))
    def _():
        ext[:, :, 0:8, :] = jnp.zeros((levels, tiles + 2, 8, LANES), F32)

    @pl.when(has_down)
    def _():
        for copy in above:
            copy.wait_recv()
        fill_rows(1, rows + 8)
        rim(rows + 8, 8, got_corner[2], got_corner[3])

    @pl.when(jnp.logical_not(has_down))
    def _():
        ext[:, :, rows + 8 : rows + 16, :] = jnp.zeros((levels, tiles + 2, 8, LANES), F32)

    for copy in flat:
        copy.wait_recv()
    rim(8, rows, got_col[0], got_col[1])

    def shift_rims(t, carry):
        for v in range(levels):
            shift_block(v, t, 0, 8)
            shift_block(v, t, rows + 8, 8)
        return carry

    edges = min(tiles, 2)
    for v in range(levels):
        shift_block(v, 0, 8, rows, (-2, -1))
        shift_block(v, tiles - 1, 8, rows, (1, 2))
    lax.fori_loop(0, tiles, shift_rims, 0)
    outer = sorted({0, groups - 1})

    def advect_rims(t, carry):
        advect(t, outer)
        return carry

    def advect_edge(n, carry):
        advect(n * (tiles - 1), range(groups))
        return carry

    lax.fori_loop(0, edges, advect_edge, 0)
    lax.fori_loop(1, tiles - 1, advect_rims, 0)

    loads[tiles + 3].wait()
    contract_last = (((1,), (1,)), ((), ()))
    send_f[...] = jnp.zeros_like(send_f)
    for v in range(levels):
        value = adv[v * rows : (v + 1) * rows, :]
        lead = value.astype(BF16)
        rest = (value - lead.astype(F32)).astype(BF16)
        both = lax.dot_general(tab[...], lead, contract_last, preferred_element_type=F32)
        more = lax.dot_general(
            tab[0 : 2 * waves, :], rest, contract_last, preferred_element_type=F32
        )
        coeffs = both[0 : 2 * waves] + both[2 * waves :] + more
        send_f[v, :, 0:rows] = coeffs[0:waves]
        send_f[v, :, HALF : HALF + rows] = coeffs[waves:]
    copies_f = []
    for d in others(e, n_lev):
        copy = remote(send_f.at[d], got_f.at[e], f_send.at[d], f_recv.at[e], l, d)
        copy.start()
        copies_f.append(copy)
    got_f[e] = send_f[e]
    for d in others(e, n_lev):
        remote(send_f.at[d], got_f.at[d], f_send.at[d], f_recv.at[d], l, d).wait_recv()
    total = got_f[0]
    for d in range(1, n_lev):
        total = total + got_f[d]
    fourier = total.astype(BF16)
    send_x[...] = fourier
    copy_x = remote(send_x, got_x, x_send, x_recv, mirror, e)
    copy_x.start()

    at_row = lax.broadcasted_iota(jnp.int32, (LANES, LANES), 0)
    at_col = lax.broadcasted_iota(jnp.int32, (LANES, LANES), 1)
    flip = ((at_row + at_col == rows - 1) & (at_row < HALF) & (at_col < HALF)) | (
        (at_row + at_col == 2 * HALF + rows - 1) & (at_row >= HALF) & (at_col >= HALF)
    )
    flip = flip.astype(F32)
    sign = jnp.where(l < n_lat // 2, 1.0, -1.0).astype(F32)
    loads[tiles + 4].wait()
    copy_x.wait_recv()
    partner = jnp.dot(got_x[...], flip.astype(BF16), preferred_element_type=F32)
    combined = partner + sign * fourier.astype(F32)

    forward_scale = 1.0 / math.sqrt(rows * n_lat // 2)
    group = 16
    for k0 in range(0, waves, group):
        ks = slice(k0, k0 + group)
        real = jnp.zeros((group, steps), F32)
        imag = jnp.zeros((group, steps), F32)
        for i in range(rows):
            values = leg[i, ks, :].astype(F32)
            real = real + values * combined[ks, i : i + 1]
            imag = imag + values * combined[ks, HALF + i : HALF + i + 1]
        sums[0, ks, :] = real * forward_scale
        sums[1, ks, :] = imag * forward_scale
    for s in range(waves):
        k = inv[s]
        chg_slot[s, 0:1, :] = sums[0, pl.ds(k, 1), :]
        chg_slot[s, 1:2, :] = sums[1, pl.ds(k, 1), :]
    send_s[...] = chg_slot[...]
    own = waves // n_lat
    copies_s = []
    for d in others(l, n_lat):
        copy = remote(
            send_s.at[pl.ds(d * own, own)], got_s.at[l], s_send.at[d], s_recv.at[l], d, e
        )
        copy.start()
        copies_s.append(copy)
    got_s[l] = send_s[pl.ds(l * own, own)]
    for d in others(l, n_lat):
        remote(
            send_s.at[pl.ds(d * own, own)], got_s.at[d], s_send.at[d], s_recv.at[d], d, e
        ).wait_recv()

    column = lax.broadcasted_iota(jnp.int32, (2, steps), 1)
    for p in range(2):
        start = p * (n_lat // 2)
        raw = got_s[start]
        for d in range(start + 1, start + n_lat // 2):
            raw = raw + got_s[d]
        for so in range(own):
            wave = inv[l * own + so] * (NT + 1) // waves
            degree = wave + 2 * column + p
            factor = 1.0 / (
                1.0 + DAMPING * (degree * (degree + 1)).astype(F32) / float(NT * (NT + 1))
            )
            masked = jnp.where(degree <= NT, raw[so], 0.0)
            damped = masked * factor
            spec_ref[so, p, 0] = damped
            send_c[p, so] = (damped - masked).astype(BF16)
    copies_c = []
    parity_of = lambda d: d // (n_lat // 2)
    for d in others(l, n_lat):
        copy = remote(send_c.at[parity_of(d)], got_c.at[l], c_send.at[d], c_recv.at[l], d, e)
        copy.start()
        copies_c.append(copy)
    got_c[l] = send_c[parity_of(l)]
    for d in others(l, n_lat):
        remote(
            send_c.at[parity_of(d)], got_c.at[d], c_send.at[d], c_recv.at[d], d, e
        ).wait_recv()

    for d in range(n_lat):
        for so in range(own):
            chg_slot[d * own + so] = got_c[d, so].astype(F32)
    for k in range(waves):
        value = chg_slot[slot_ref[k]]
        chg[0, k : k + 1, :] = value[0:1]
        chg[1, k : k + 1, :] = value[1:2]
    inverse_scale = math.sqrt(NLON) / math.sqrt(waves) / math.sqrt(steps)
    lane = lax.broadcasted_iota(jnp.int32, (group, LANES), 1)
    wave_row = lax.broadcasted_iota(jnp.int32, (group, LANES), 0)
    for k0 in range(0, waves, group):
        ks = slice(k0, k0 + group)
        real, imag = chg[0, ks, :], chg[1, ks, :]
        half = jnp.zeros((group, LANES), F32)
        for i in range(rows):
            values = leg[i, ks, :].astype(F32)
            half = jnp.where(lane == i, jnp.sum(values * real, axis=1, keepdims=True), half)
            half = jnp.where(
                lane == HALF + i, jnp.sum(values * imag, axis=1, keepdims=True), half
            )
        half = half * jnp.where(wave_row + k0 == 0, inverse_scale, 2.0 * inverse_scale)
        send_h[0, ks, :] = half
        send_h[1, ks, :] = jnp.dot(
            half, flip, precision=lax.Precision.HIGHEST, preferred_element_type=F32
        )
    copies_h = []
    for off in range(n_lev):
        d = lax.rem(e + off, n_lev)
        copy = remote(send_h.at[1], got_h.at[1, e], h_send.at[1, d], h_recv.at[1, e], mirror, d)
        copy.start()
        copies_h.append(copy)
    for d in others(e, n_lev):
        copy = remote(send_h.at[0], got_h.at[0, e], h_send.at[0, d], h_recv.at[0, e], l, d)
        copy.start()
        copies_h.append(copy)
    got_h[0, e] = send_h[0]
    for d in others(e, n_lev):
        remote(
            send_h.at[0], got_h.at[0, d], h_send.at[0, d], h_recv.at[0, d], l, d
        ).wait_recv()
    for off in range(n_lev):
        d = lax.rem(e + off, n_lev)
        remote(
            send_h.at[1], got_h.at[1, d], h_send.at[1, d], h_recv.at[1, d], mirror, d
        ).wait_recv()

    stack = []
    for v in range(levels):
        synthesis = got_h[1, v] + sign * got_h[0, v]
        both = jnp.concatenate([synthesis, pltpu.roll(synthesis, HALF, 1)], axis=0)
        stack.append(jnp.transpose(both)[0:rows, :])
    synthesis = jnp.concatenate(stack, axis=0)
    lead = synthesis.astype(BF16)
    rest = (synthesis - lead.astype(F32)).astype(BF16)
    chunk = min(width, 256)
    for j in range(0, width, chunk):
        cols = slice(j, j + chunk)
        table, table_rest = tab[0 : 2 * waves, cols], tab[2 * waves :, cols]
        increment = (
            jnp.dot(lead, table, preferred_element_type=F32)
            + jnp.dot(lead, table_rest, preferred_element_type=F32)
            + jnp.dot(rest, table, preferred_element_type=F32)
        )
        updated = adv[:, cols] + increment
        for v in range(levels):
            out_ref[v, :, cols] = updated[v * rows : (v + 1) * rows]

    for copy in flat + copies_f + [copy_x] + copies_s + copies_c + copies_h:
        copy.wait_send()

    @pl.when(has_down)
    def _():
        for copy in below:
            copy.wait_send()

    @pl.when(has_up)
    def _():
        for copy in above:
            copy.wait_send()


def solution(mesh):
    n_lat, n_lev = mesh.shape["lat"], mesh.shape["lev"]

    def on_device(field, weights, depart_row, depart_col, legendre, wave_slot):
        levels, rows, width = field.shape
        _, waves, steps = legendre.shape
        tiles = width // LANES
        own = waves // n_lat
        table = jnp.asarray(lon_table(waves))
        vmem, dma = pltpu.VMEM, pltpu.SemaphoreType.DMA
        anywhere = pl.BlockSpec(memory_space=pltpu.HBM)
        in_vmem = pl.BlockSpec(memory_space=pltpu.VMEM)
        return pl.pallas_call(
            functools.partial(kernel, n_lat, n_lev),
            out_shape=(
                jax.ShapeDtypeStruct((levels, rows, width), F32),
                jax.ShapeDtypeStruct((own, 2, 1, 2, steps), F32),
            ),
            in_specs=[pl.BlockSpec(memory_space=pltpu.SMEM)] + [anywhere] * 6,
            out_specs=(in_vmem, in_vmem),
            scratch_shapes=[
                vmem((levels, tiles + 2, rows + 16, LANES), F32),
                vmem((4, levels, tiles, rows + 16, LANES), F32),
                vmem((4, rows, width), BF16),
                vmem((rows, width), jnp.int32),
                vmem((rows, width), jnp.int32),
                vmem((rows, waves, steps), BF16),
                vmem((4 * waves, width), BF16),
                vmem((levels * rows, width), F32),
                pltpu.SMEM((waves,), jnp.int32),
                vmem((2, 2 * levels, width), F32),
                vmem((2, rows, LANES), F32),
                vmem((2, 2 * levels, width), F32),
                vmem((2, rows, LANES), F32),
                vmem((4, 8, LANES), F32),
                vmem((n_lev, waves, LANES), F32),
                vmem((n_lev, waves, LANES), F32),
                vmem((waves, LANES), BF16),
                vmem((waves, LANES), BF16),
                vmem((2, waves, steps), F32),
                vmem((waves, 2, steps), F32),
                vmem((n_lat, own, 2, steps), F32),
                vmem((2, own, 2, steps), BF16),
                vmem((n_lat, own, 2, steps), BF16),
                vmem((waves, 2, steps), F32),
                vmem((2, waves, steps), F32),
                vmem((2, waves, LANES), F32),
                vmem((2, n_lev, waves, LANES), F32),
                dma((tiles + 5,)),
                dma((8,)), dma((8,)),
                dma((n_lev,)), dma((n_lev,)),
                dma, dma,
                dma((n_lat,)), dma((n_lat,)),
                dma((n_lat,)), dma((n_lat,)),
                dma((2, n_lev)), dma((2, n_lev)),
            ],
            compiler_params=pltpu.CompilerParams(
                collective_id=0, has_side_effects=True, vmem_limit_bytes=32 << 20
            ),
        )(wave_slot, field, weights, depart_row, depart_col, legendre, table)

    placed = (
        P(None, "lat", "lev"),
        P(None, "lat", "lev"),
        P("lat", "lev"),
        P("lat", "lev"),
        P("lat", None, None),
        P(),
    )
    return jax.shard_map(
        on_device,
        mesh=mesh,
        in_specs=placed,
        out_specs=(P(None, "lat", "lev"), P("lat", None, "lev", None, None)),
        check_vma=False,
    )
```

```python
import functools
import math

import jax
import jax.numpy as jnp
import numpy as np
from jax import lax
from jax.experimental import pallas as pl
from jax.experimental.pallas import tpu as pltpu
from jax.sharding import PartitionSpec as P

NLON = 4096
NT = 1279
DAMPING = 4.0
LANES = 128
HALF = 64
MESH = pl.DeviceIdType.MESH
F32 = jnp.float32
BF16 = jnp.bfloat16


def lon_table(waves):
    m = (np.arange(waves, dtype=np.int64) * (NT + 1)) // waves
    phases = (m[:, None] * np.arange(NLON, dtype=np.int64)[None, :]) % NLON
    angles = phases.astype(np.float64) * (2.0 * math.pi / NLON)
    table = np.concatenate([np.cos(angles), -np.sin(angles)], axis=0) / math.sqrt(NLON)
    table = table.astype(np.float32)
    lead = table.astype(BF16)
    rest = (table - lead.astype(np.float32)).astype(BF16)
    return np.concatenate([lead, rest], axis=0)


def kernel(
    n_lat, n_lev,
    slot_ref, field_hbm, weights_hbm, drow_hbm, dcol_hbm, leg_hbm, table_hbm,
    out_ref, spec_ref, adv_hbm,
    ext, shifted, wts, drow, dcol, leg, tab, adv, inv,
    pack_row, pack_col, got_row, got_col, got_corner,
    send_f, got_f, send_x, got_x, sums, send_s, got_s, send_c, got_c,
    chg_slot, chg, send_h, got_h,
    load_sem, adv_sem, halo_send, halo_recv, f_send, f_recv, x_send, x_recv,
    s_send, s_recv, c_send, c_recv, h_send, h_recv,
):
    levels, rows, width = out_ref.shape
    tiles = width // LANES
    waves, steps = leg.shape[1], leg.shape[2]
    l, e = lax.axis_index("lat"), lax.axis_index("lev")
    mirror = n_lat - 1 - l
    has_up, has_down = l > 0, l < n_lat - 1
    east, west = lax.rem(e + 1, n_lev), lax.rem(e + n_lev - 1, n_lev)
    others = lambda start, size: [lax.rem(start + off, size) for off in range(1, size)]

    loads = []

    def load(src, dst):
        copy = pltpu.make_async_copy(src, dst, load_sem.at[len(loads)])
        copy.start()
        loads.append(copy)

    for t in range(tiles):
        load(
            field_hbm.at[:, :, pl.ds(t * LANES, LANES)],
            ext.at[:, t + 1, pl.ds(8, rows), :],
        )
    load(weights_hbm, wts)
    load(drow_hbm, drow)
    load(dcol_hbm, dcol)
    load(table_hbm.at[:, pl.ds(pl.multiple_of(e * width, LANES), width)], tab)
    load(leg_hbm, leg)

    barrier = pltpu.get_barrier_semaphore()

    def greet(lat, lev):
        pl.semaphore_signal(barrier, inc=1, device_id=(lat, lev), device_id_type=MESH)

    for d in others(l, n_lat):
        greet(d, e)
    for d in others(e, n_lev):
        greet(l, d)
        greet(mirror, d)

    @pl.when(has_up)
    def _():
        greet(l - 1, east)
        greet(l - 1, west)

    @pl.when(has_down)
    def _():
        greet(l + 1, east)
        greet(l + 1, west)

    lane = lax.broadcasted_iota(jnp.int32, (rows, LANES), 1)
    for t in range(tiles):
        loads[t].wait()
    for v in range(levels):
        for t in range(tiles):
            cols = slice(t * LANES, (t + 1) * LANES)
            pack_row[0, 2 * v : 2 * v + 2, cols] = ext[v, t + 1, 6 + rows : 8 + rows, :]
            pack_row[1, 2 * v : 2 * v + 2, cols] = ext[v, t + 1, 8:10, :]
    last = jnp.zeros((rows, LANES), F32)
    first = jnp.zeros((rows, LANES), F32)
    for v in range(levels):
        here = (lane == 2 * v) | (lane == 2 * v + 1)
        tail = pltpu.roll(ext[v, tiles, 8 : 8 + rows, :], (2 * v + 2) % LANES, 1)
        last = jnp.where(here, tail, last)
        head = ext[v, 1, 8 : 8 + rows, :]
        if v:
            head = pltpu.roll(head, 2 * v, 1)
        first = jnp.where(here, head, first)
    pack_col[0] = last
    pack_col[1] = first

    def shift_block(v, t, row0, size, moves=(-2, -1, 1, 2)):
        at = pl.ds(row0, size)
        at_lane = lax.broadcasted_iota(jnp.int32, (size, LANES), 1)
        here = ext[v, t + 1, at, :]
        left = ext[v, t, at, :] if min(moves) < 0 else None
        right = ext[v, t + 2, at, :] if max(moves) > 0 else None
        for move in moves:
            n_move = (-2, -1, 1, 2).index(move)
            amount = (-move) % LANES
            mine = pltpu.roll(here, amount, 1)
            if move < 0:
                moved = jnp.where(at_lane < -move, pltpu.roll(left, amount, 1), mine)
            else:
                moved = jnp.where(at_lane >= LANES - move, pltpu.roll(right, amount, 1), mine)
            shifted[n_move, v, t, at, :] = moved

    def shift_inner(chosen):
        def step(t, carry):
            for v in chosen:
                shift_block(v, t, 8, rows)
            return carry

        lax.fori_loop(1, tiles - 1, step, 0)

    groups = rows // 8

    def advect(t, chosen):
        cols = pl.ds(pl.multiple_of(t * LANES, LANES), LANES)
        corner = [wts[ab, :, cols].astype(F32) for ab in range(4)]
        for g in chosen:
            band = slice(8 * g, 8 * g + 8)
            dr, dc = drow[band, cols], dcol[band, cols]
            zero = jnp.zeros((8, LANES), F32)
            in_col = {c: dc == c for c in range(-2, 2)}
            in_row = {r: dr == r for r in range(-2, 2)}

            def pick(masks, at, one, two):
                value = zero
                if at - 1 in masks:
                    value = jnp.where(masks[at - 1], two, value)
                if at in masks:
                    value = jnp.where(masks[at], one, value)
                return value

            part = [
                [pick(in_col, c, corner[2 * a][band], corner[2 * a + 1][band]) for c in range(-2, 3)]
                for a in range(2)
            ]
            coef = [
                [pick(in_row, r, part[0][c], part[1][c]) for c in range(5)] for r in range(-2, 3)
            ]
            for v in range(levels):
                total = None
                for r in range(5):
                    at = pl.ds(8 * g + 6 + r, 8)
                    for c in range(5):
                        if c == 2:
                            value = ext[v, t + 1, at, :]
                        else:
                            value = shifted[c if c < 2 else c - 1, v, t, at, :]
                        term = coef[r][c] * value
                        total = term if total is None else total + term
                adv[v * rows + 8 * g : v * rows + 8 * g + 8, cols] = total

    def advect_inner(t, carry):
        advect(t, range(1, groups - 1))
        return carry

    shift_inner(range(levels // 2))

    n_greet = (n_lat - 1) + 2 * (n_lev - 1)
    n_greet = n_greet + jnp.where(has_up, 2, 0) + jnp.where(has_down, 2, 0)
    pl.semaphore_wait(barrier, n_greet)

    def remote(src, dst, ssem, rsem, lat, lev):
        return pltpu.make_async_remote_copy(
            src_ref=src, dst_ref=dst, send_sem=ssem, recv_sem=rsem,
            device_id=(lat, lev), device_id_type=MESH,
        )

    def halo(n, src, dst, lat, lev):
        return remote(src, dst, halo_send.at[n], halo_recv.at[n], lat, lev)

    bottom, top = pl.ds(rows - 8, 8), pl.ds(0, 8)
    flat = [
        halo(0, pack_col.at[0], got_col.at[0], l, east),
        halo(1, pack_col.at[1], got_col.at[1], l, west),
    ]
    below = [
        halo(2, pack_row.at[0], got_row.at[0], l + 1, e),
        halo(3, pack_col.at[0, bottom], got_corner.at[0], l + 1, east),
        halo(4, pack_col.at[1, bottom], got_corner.at[1], l + 1, west),
    ]
    above = [
        halo(5, pack_row.at[1], got_row.at[1], l - 1, e),
        halo(6, pack_col.at[0, top], got_corner.at[2], l - 1, east),
        halo(7, pack_col.at[1, top], got_corner.at[3], l - 1, west),
    ]

    @pl.when(has_down)
    def _():
        for copy in below:
            copy.start()

    @pl.when(has_up)
    def _():
        for copy in above:
            copy.start()

    for copy in flat:
        copy.start()

    def find(s, carry):
        def step(k, found):
            return jnp.where(slot_ref[k] == s, k, found)

        inv[s] = lax.fori_loop(0, waves, step, jnp.int32(0))
        return carry

    lax.fori_loop(0, waves, find, 0)

    shift_inner(range(levels // 2, levels))
    if tiles > 1:
        for v in range(levels):
            shift_block(v, 0, 8, rows, (1, 2))
            shift_block(v, tiles - 1, 8, rows, (-2, -1))
    for n in range(tiles, tiles + 3):
        loads[n].wait()
    lax.fori_loop(1, tiles - 1, advect_inner, 0)

    def spread(piece, v):
        return pltpu.roll(piece, LANES - 2 - 2 * v, 1)

    def spread_east(piece, v):
        return pltpu.roll(piece, LANES - 2 * v, 1) if v else piece

    def rim(row0, size, from_west, from_east):
        for v in range(levels):
            ext[v, 0, row0 : row0 + size, :] = spread(from_west, v)
            ext[v, tiles + 1, row0 : row0 + size, :] = spread_east(from_east, v)

    def fill_rows(which, row0):
        for v in range(levels):
            for t in range(tiles):
                cols = slice(t * LANES, (t + 1) * LANES)
                ext[v, t + 1, row0 : row0 + 2, :] = got_row[which, 2 * v : 2 * v + 2, cols]

    @pl.when(has_up)
    def _():
        for copy in below:
            copy.wait_recv()
        fill_rows(0, 6)
        rim(0, 8, got_corner[0], got_corner[1])

    @pl.when(jnp.logical_not(has_up))
    def _():
        ext[:, :, 0:8, :] = jnp.zeros((levels, tiles + 2, 8, LANES), F32)

    @pl.when(has_down)
    def _():
        for copy in above:
            copy.wait_recv()
        fill_rows(1, rows + 8)
        rim(rows + 8, 8, got_corner[2], got_corner[3])

    @pl.when(jnp.logical_not(has_down))
    def _():
        ext[:, :, rows + 8 : rows + 16, :] = jnp.zeros((levels, tiles + 2, 8, LANES), F32)

    for copy in flat:
        copy.wait_recv()
    rim(8, rows, got_col[0], got_col[1])

    def shift_rims(t, carry):
        for v in range(levels):
            shift_block(v, t, 0, 8)
            shift_block(v, t, rows + 8, 8)
        return carry

    edges = min(tiles, 2)
    for v in range(levels):
        shift_block(v, 0, 8, rows, (-2, -1))
        shift_block(v, tiles - 1, 8, rows, (1, 2))
    lax.fori_loop(0, tiles, shift_rims, 0)
    outer = sorted({0, groups - 1})

    def advect_rims(t, carry):
        advect(t, outer)
        return carry

    def advect_edge(n, carry):
        advect(n * (tiles - 1), range(groups))
        return carry

    lax.fori_loop(0, edges, advect_edge, 0)
    lax.fori_loop(1, tiles - 1, advect_rims, 0)

    copies_adv = []
    for v in range(levels):
        copy = pltpu.make_async_copy(
            adv.at[pl.ds(v * rows, rows), :], adv_hbm.at[v], adv_sem.at[v]
        )
        copy.start()
        copies_adv.append(copy)

    loads[tiles + 3].wait()
    contract_last = (((1,), (1,)), ((), ()))
    send_f[...] = jnp.zeros_like(send_f)
    for v in range(levels):
        value = adv[v * rows : (v + 1) * rows, :]
        lead = value.astype(BF16)
        rest = (value - lead.astype(F32)).astype(BF16)
        both = lax.dot_general(tab[...], lead, contract_last, preferred_element_type=F32)
        more = lax.dot_general(
            tab[0 : 2 * waves, :], rest, contract_last, preferred_element_type=F32
        )
        coeffs = both[0 : 2 * waves] + both[2 * waves :] + more
        send_f[v, :, 0:rows] = coeffs[0:waves]
        send_f[v, :, HALF : HALF + rows] = coeffs[waves:]
    copies_f = []
    for d in others(e, n_lev):
        copy = remote(send_f.at[d], got_f.at[e], f_send.at[d], f_recv.at[e], l, d)
        copy.start()
        copies_f.append(copy)
    got_f[e] = send_f[e]
    for d in others(e, n_lev):
        remote(send_f.at[d], got_f.at[d], f_send.at[d], f_recv.at[d], l, d).wait_recv()
    total = got_f[0]
    for d in range(1, n_lev):
        total = total + got_f[d]
    fourier = total.astype(BF16)
    send_x[...] = fourier
    copy_x = remote(send_x, got_x, x_send, x_recv, mirror, e)
    copy_x.start()

    at_row = lax.broadcasted_iota(jnp.int32, (LANES, LANES), 0)
    at_col = lax.broadcasted_iota(jnp.int32, (LANES, LANES), 1)
    flip = ((at_row + at_col == rows - 1) & (at_row < HALF) & (at_col < HALF)) | (
        (at_row + at_col == 2 * HALF + rows - 1) & (at_row >= HALF) & (at_col >= HALF)
    )
    flip = flip.astype(F32)
    sign = jnp.where(l < n_lat // 2, 1.0, -1.0).astype(F32)
    loads[tiles + 4].wait()
    copy_x.wait_recv()
    partner = jnp.dot(got_x[...], flip.astype(BF16), preferred_element_type=F32)
    combined = partner + sign * fourier.astype(F32)

    forward_scale = 1.0 / math.sqrt(rows * n_lat // 2)
    group = 16
    for k0 in range(0, waves, group):
        ks = slice(k0, k0 + group)
        real = jnp.zeros((group, steps), F32)
        imag = jnp.zeros((group, steps), F32)
        for i in range(rows):
            values = leg[i, ks, :].astype(F32)
            real = real + values * combined[ks, i : i + 1]
            imag = imag + values * combined[ks, HALF + i : HALF + i + 1]
        sums[0, ks, :] = real * forward_scale
        sums[1, ks, :] = imag * forward_scale
    for s in range(waves):
        k = inv[s]
        chg_slot[s, 0:1, :] = sums[0, pl.ds(k, 1), :]
        chg_slot[s, 1:2, :] = sums[1, pl.ds(k, 1), :]
    send_s[...] = chg_slot[...]
    own = waves // n_lat
    copies_s = []
    for d in others(l, n_lat):
        copy = remote(
            send_s.at[pl.ds(d * own, own)], got_s.at[l], s_send.at[d], s_recv.at[l], d, e
        )
        copy.start()
        copies_s.append(copy)
    got_s[l] = send_s[pl.ds(l * own, own)]
    for d in others(l, n_lat):
        remote(
            send_s.at[pl.ds(d * own, own)], got_s.at[d], s_send.at[d], s_recv.at[d], d, e
        ).wait_recv()

    column = lax.broadcasted_iota(jnp.int32, (2, steps), 1)
    for p in range(2):
        start = p * (n_lat // 2)
        raw = got_s[start]
        for d in range(start + 1, start + n_lat // 2):
            raw = raw + got_s[d]
        for so in range(own):
            wave = inv[l * own + so] * (NT + 1) // waves
            degree = wave + 2 * column + p
            factor = 1.0 / (
                1.0 + DAMPING * (degree * (degree + 1)).astype(F32) / float(NT * (NT + 1))
            )
            masked = jnp.where(degree <= NT, raw[so], 0.0)
            damped = masked * factor
            spec_ref[so, p, 0] = damped
            send_c[p, so] = (damped - masked).astype(BF16)
    copies_c = []
    parity_of = lambda d: d // (n_lat // 2)
    for d in others(l, n_lat):
        copy = remote(send_c.at[parity_of(d)], got_c.at[l], c_send.at[d], c_recv.at[l], d, e)
        copy.start()
        copies_c.append(copy)
    got_c[l] = send_c[parity_of(l)]
    for d in others(l, n_lat):
        remote(
            send_c.at[parity_of(d)], got_c.at[d], c_send.at[d], c_recv.at[d], d, e
        ).wait_recv()

    for d in range(n_lat):
        for so in range(own):
            chg_slot[d * own + so] = got_c[d, so].astype(F32)
    for k in range(waves):
        value = chg_slot[slot_ref[k]]
        chg[0, k : k + 1, :] = value[0:1]
        chg[1, k : k + 1, :] = value[1:2]
    inverse_scale = math.sqrt(NLON) / math.sqrt(waves) / math.sqrt(steps)
    lane = lax.broadcasted_iota(jnp.int32, (group, LANES), 1)
    wave_row = lax.broadcasted_iota(jnp.int32, (group, LANES), 0)
    for k0 in range(0, waves, group):
        ks = slice(k0, k0 + group)
        real, imag = chg[0, ks, :], chg[1, ks, :]
        half = jnp.zeros((group, LANES), F32)
        for i in range(rows):
            values = leg[i, ks, :].astype(F32)
            half = jnp.where(lane == i, jnp.sum(values * real, axis=1, keepdims=True), half)
            half = jnp.where(
                lane == HALF + i, jnp.sum(values * imag, axis=1, keepdims=True), half
            )
        half = half * jnp.where(wave_row + k0 == 0, inverse_scale, 2.0 * inverse_scale)
        send_h[0, ks, :] = half
        send_h[1, ks, :] = jnp.dot(
            half, flip, precision=lax.Precision.HIGHEST, preferred_element_type=F32
        )
    copies_h = []
    for off in range(n_lev):
        d = lax.rem(e + off, n_lev)
        copy = remote(send_h.at[1], got_h.at[1, e], h_send.at[1, d], h_recv.at[1, e], mirror, d)
        copy.start()
        copies_h.append(copy)
    for d in others(e, n_lev):
        copy = remote(send_h.at[0], got_h.at[0, e], h_send.at[0, d], h_recv.at[0, e], l, d)
        copy.start()
        copies_h.append(copy)
    got_h[0, e] = send_h[0]
    for d in others(e, n_lev):
        remote(
            send_h.at[0], got_h.at[0, d], h_send.at[0, d], h_recv.at[0, d], l, d
        ).wait_recv()
    for off in range(n_lev):
        d = lax.rem(e + off, n_lev)
        remote(
            send_h.at[1], got_h.at[1, d], h_send.at[1, d], h_recv.at[1, d], mirror, d
        ).wait_recv()

    stack = []
    for v in range(levels):
        synthesis = got_h[1, v] + sign * got_h[0, v]
        both = jnp.concatenate([synthesis, pltpu.roll(synthesis, HALF, 1)], axis=0)
        stack.append(jnp.transpose(both)[0:rows, :])
    synthesis = jnp.concatenate(stack, axis=0)
    lead = synthesis.astype(BF16)
    rest = (synthesis - lead.astype(F32)).astype(BF16)
    chunk = min(width, 256)
    for j in range(0, width, chunk):
        cols = slice(j, j + chunk)
        table, table_rest = tab[0 : 2 * waves, cols], tab[2 * waves :, cols]
        increment = (
            jnp.dot(lead, table, preferred_element_type=F32)
            + jnp.dot(lead, table_rest, preferred_element_type=F32)
            + jnp.dot(rest, table, preferred_element_type=F32)
        )
        for v in range(levels):
            out_ref[v, :, cols] = increment[v * rows : (v + 1) * rows]

    for copy in copies_adv:
        copy.wait()
    for copy in flat + copies_f + [copy_x] + copies_s + copies_c + copies_h:
        copy.wait_send()

    @pl.when(has_down)
    def _():
        for copy in below:
            copy.wait_send()

    @pl.when(has_up)
    def _():
        for copy in above:
            copy.wait_send()


def solution(mesh):
    n_lat, n_lev = mesh.shape["lat"], mesh.shape["lev"]

    def on_device(field, weights, depart_row, depart_col, legendre, wave_slot):
        levels, rows, width = field.shape
        _, waves, steps = legendre.shape
        tiles = width // LANES
        own = waves // n_lat
        table = jnp.asarray(lon_table(waves))
        vmem, dma = pltpu.VMEM, pltpu.SemaphoreType.DMA
        anywhere = pl.BlockSpec(memory_space=pltpu.HBM)
        in_vmem = pl.BlockSpec(memory_space=pltpu.VMEM)
        increment, spectral, advected = pl.pallas_call(
            functools.partial(kernel, n_lat, n_lev),
            out_shape=(
                jax.ShapeDtypeStruct((levels, rows, width), F32),
                jax.ShapeDtypeStruct((own, 2, 1, 2, steps), F32),
                jax.ShapeDtypeStruct((levels, rows, width), F32),
            ),
            in_specs=[pl.BlockSpec(memory_space=pltpu.SMEM)] + [anywhere] * 6,
            out_specs=(in_vmem, in_vmem, anywhere),
            scratch_shapes=[
                vmem((levels, tiles + 2, rows + 16, LANES), F32),
                vmem((4, levels, tiles, rows + 16, LANES), F32),
                vmem((4, rows, width), BF16),
                vmem((rows, width), jnp.int32),
                vmem((rows, width), jnp.int32),
                vmem((rows, waves, steps), BF16),
                vmem((4 * waves, width), BF16),
                vmem((levels * rows, width), F32),
                pltpu.SMEM((waves,), jnp.int32),
                vmem((2, 2 * levels, width), F32),
                vmem((2, rows, LANES), F32),
                vmem((2, 2 * levels, width), F32),
                vmem((2, rows, LANES), F32),
                vmem((4, 8, LANES), F32),
                vmem((n_lev, waves, LANES), F32),
                vmem((n_lev, waves, LANES), F32),
                vmem((waves, LANES), BF16),
                vmem((waves, LANES), BF16),
                vmem((2, waves, steps), F32),
                vmem((waves, 2, steps), F32),
                vmem((n_lat, own, 2, steps), F32),
                vmem((2, own, 2, steps), BF16),
                vmem((n_lat, own, 2, steps), BF16),
                vmem((waves, 2, steps), F32),
                vmem((2, waves, steps), F32),
                vmem((2, waves, LANES), F32),
                vmem((2, n_lev, waves, LANES), F32),
                dma((tiles + 5,)), dma((levels,)),
                dma((8,)), dma((8,)),
                dma((n_lev,)), dma((n_lev,)),
                dma, dma,
                dma((n_lat,)), dma((n_lat,)),
                dma((n_lat,)), dma((n_lat,)),
                dma((2, n_lev)), dma((2, n_lev)),
            ],
            compiler_params=pltpu.CompilerParams(
                collective_id=0, has_side_effects=True, vmem_limit_bytes=63 << 20
            ),
        )(wave_slot, field, weights, depart_row, depart_col, legendre, table)
        return (advected + increment, spectral)

    placed = (
        P(None, "lat", "lev"),
        P(None, "lat", "lev"),
        P("lat", "lev"),
        P("lat", "lev"),
        P("lat", None, None),
        P(),
    )
    return jax.shard_map(
        on_device,
        mesh=mesh,
        in_specs=placed,
        out_specs=(P(None, "lat", "lev"), P("lat", None, "lev", None, None)),
        check_vma=False,
    )
```

```python
import functools
import math

import jax
import jax.numpy as jnp
import numpy as np
from jax import lax
from jax.experimental import pallas as pl
from jax.experimental.pallas import tpu as pltpu
from jax.sharding import PartitionSpec as P

NLON = 4096
NT = 1279
DAMPING = 4.0
LANES = 128
HALF = 64
MESH = pl.DeviceIdType.MESH
F32 = jnp.float32
BF16 = jnp.bfloat16


def lon_table(waves):
    m = (np.arange(waves, dtype=np.int64) * (NT + 1)) // waves
    phases = (m[:, None] * np.arange(NLON, dtype=np.int64)[None, :]) % NLON
    angles = phases.astype(np.float64) * (2.0 * math.pi / NLON)
    table = np.concatenate([np.cos(angles), -np.sin(angles)], axis=0) / math.sqrt(NLON)
    table = table.astype(np.float32)
    lead = table.astype(BF16)
    rest = (table - lead.astype(np.float32)).astype(BF16)
    return np.concatenate([lead, rest], axis=0)


def kernel(
    n_lat, n_lev,
    slot_ref, field_hbm, weights_hbm, drow_hbm, dcol_hbm, leg_hbm, table_hbm,
    out_ref, spec_ref,
    ext, shifted, wts, drow, dcol, leg, tab, adv, inv,
    pack_row, pack_col, got_row, got_col, got_corner,
    send_f, got_f, send_x, got_x, sums, send_s, got_s, send_c, got_c,
    chg_slot, chg, send_h, got_h,
    load_sem, halo_send, halo_recv, f_send, f_recv, x_send, x_recv,
    s_send, s_recv, c_send, c_recv, h_send, h_recv,
):
    levels, rows, width = out_ref.shape
    tiles = width // LANES
    waves, steps = leg.shape[1], leg.shape[2]
    l, e = lax.axis_index("lat"), lax.axis_index("lev")
    mirror = n_lat - 1 - l
    has_up, has_down = l > 0, l < n_lat - 1
    east, west = lax.rem(e + 1, n_lev), lax.rem(e + n_lev - 1, n_lev)
    others = lambda start, size: [lax.rem(start + off, size) for off in range(1, size)]

    loads = []

    def load(src, dst):
        copy = pltpu.make_async_copy(src, dst, load_sem.at[len(loads)])
        copy.start()
        loads.append(copy)

    for t in range(tiles):
        load(
            field_hbm.at[:, :, pl.ds(t * LANES, LANES)],
            ext.at[:, t + 1, pl.ds(8, rows), :],
        )
    load(weights_hbm, wts)
    load(drow_hbm, drow)
    load(dcol_hbm, dcol)
    load(table_hbm.at[:, pl.ds(pl.multiple_of(e * width, LANES), width)], tab)
    load(leg_hbm, leg)

    barrier = pltpu.get_barrier_semaphore()

    def greet(lat, lev):
        pl.semaphore_signal(barrier, inc=1, device_id=(lat, lev), device_id_type=MESH)

    for d in others(l, n_lat):
        greet(d, e)
    for d in others(e, n_lev):
        greet(l, d)
        greet(mirror, d)

    @pl.when(has_up)
    def _():
        greet(l - 1, east)
        greet(l - 1, west)

    @pl.when(has_down)
    def _():
        greet(l + 1, east)
        greet(l + 1, west)

    lane = lax.broadcasted_iota(jnp.int32, (rows, LANES), 1)
    for t in range(tiles):
        loads[t].wait()
    for v in range(levels):
        for t in range(tiles):
            cols = slice(t * LANES, (t + 1) * LANES)
            pack_row[0, 2 * v : 2 * v + 2, cols] = ext[v, t + 1, 6 + rows : 8 + rows, :]
            pack_row[1, 2 * v : 2 * v + 2, cols] = ext[v, t + 1, 8:10, :]
    last = jnp.zeros((rows, LANES), F32)
    first = jnp.zeros((rows, LANES), F32)
    for v in range(levels):
        here = (lane == 2 * v) | (lane == 2 * v + 1)
        tail = pltpu.roll(ext[v, tiles, 8 : 8 + rows, :], (2 * v + 2) % LANES, 1)
        last = jnp.where(here, tail, last)
        head = ext[v, 1, 8 : 8 + rows, :]
        if v:
            head = pltpu.roll(head, 2 * v, 1)
        first = jnp.where(here, head, first)
    pack_col[0] = last
    pack_col[1] = first

    def shift_block(v, t, row0, size, moves=(-2, -1, 1, 2)):
        at = pl.ds(row0, size)
        at_lane = lax.broadcasted_iota(jnp.int32, (size, LANES), 1)
        here = ext[v, t + 1, at, :]
        left = ext[v, t, at, :] if min(moves) < 0 else None
        right = ext[v, t + 2, at, :] if max(moves) > 0 else None
        for move in moves:
            n_move = (-2, -1, 1, 2).index(move)
            amount = (-move) % LANES
            mine = pltpu.roll(here, amount, 1)
            if move < 0:
                moved = jnp.where(at_lane < -move, pltpu.roll(left, amount, 1), mine)
            else:
                moved = jnp.where(at_lane >= LANES - move, pltpu.roll(right, amount, 1), mine)
            shifted[n_move, v, t, at, :] = moved

    def shift_inner(chosen):
        def step(t, carry):
            for v in chosen:
                shift_block(v, t, 8, rows)
            return carry

        lax.fori_loop(1, tiles - 1, step, 0)

    groups = rows // 8

    def advect(t, chosen):
        cols = pl.ds(pl.multiple_of(t * LANES, LANES), LANES)
        corner = [wts[ab, :, cols].astype(F32) for ab in range(4)]
        for g in chosen:
            band = slice(8 * g, 8 * g + 8)
            dr, dc = drow[band, cols], dcol[band, cols]
            zero = jnp.zeros((8, LANES), F32)
            in_col = {c: dc == c for c in range(-2, 2)}
            in_row = {r: dr == r for r in range(-2, 2)}

            def pick(masks, at, one, two):
                value = zero
                if at - 1 in masks:
                    value = jnp.where(masks[at - 1], two, value)
                if at in masks:
                    value = jnp.where(masks[at], one, value)
                return value

            part = [
                [pick(in_col, c, corner[2 * a][band], corner[2 * a + 1][band]) for c in range(-2, 3)]
                for a in range(2)
            ]
            coef = [
                [pick(in_row, r, part[0][c], part[1][c]) for c in range(5)] for r in range(-2, 3)
            ]
            for v in range(levels):
                total = None
                for r in range(5):
                    at = pl.ds(8 * g + 6 + r, 8)
                    for c in range(5):
                        if c == 2:
                            value = ext[v, t + 1, at, :]
                        else:
                            value = shifted[c if c < 2 else c - 1, v, t, at, :]
                        term = coef[r][c] * value
                        total = term if total is None else total + term
                adv[v * rows + 8 * g : v * rows + 8 * g + 8, cols] = total

    def advect_inner(t, carry):
        advect(t, range(1, groups - 1))
        return carry

    shift_inner(range(levels // 2))

    n_greet = (n_lat - 1) + 2 * (n_lev - 1)
    n_greet = n_greet + jnp.where(has_up, 2, 0) + jnp.where(has_down, 2, 0)
    pl.semaphore_wait(barrier, n_greet)

    def remote(src, dst, ssem, rsem, lat, lev):
        return pltpu.make_async_remote_copy(
            src_ref=src, dst_ref=dst, send_sem=ssem, recv_sem=rsem,
            device_id=(lat, lev), device_id_type=MESH,
        )

    def halo(n, src, dst, lat, lev):
        return remote(src, dst, halo_send.at[n], halo_recv.at[n], lat, lev)

    bottom, top = pl.ds(rows - 8, 8), pl.ds(0, 8)
    flat = [
        halo(0, pack_col.at[0], got_col.at[0], l, east),
        halo(1, pack_col.at[1], got_col.at[1], l, west),
    ]
    below = [
        halo(2, pack_row.at[0], got_row.at[0], l + 1, e),
        halo(3, pack_col.at[0, bottom], got_corner.at[0], l + 1, east),
        halo(4, pack_col.at[1, bottom], got_corner.at[1], l + 1, west),
    ]
    above = [
        halo(5, pack_row.at[1], got_row.at[1], l - 1, e),
        halo(6, pack_col.at[0, top], got_corner.at[2], l - 1, east),
        halo(7, pack_col.at[1, top], got_corner.at[3], l - 1, west),
    ]

    @pl.when(has_down)
    def _():
        for copy in below:
            copy.start()

    @pl.when(has_up)
    def _():
        for copy in above:
            copy.start()

    for copy in flat:
        copy.start()

    def find(s, carry):
        def step(k, found):
            return jnp.where(slot_ref[k] == s, k, found)

        inv[s] = lax.fori_loop(0, waves, step, jnp.int32(0))
        return carry

    lax.fori_loop(0, waves, find, 0)

    shift_inner(range(levels // 2, levels))
    if tiles > 1:
        for v in range(levels):
            shift_block(v, 0, 8, rows, (1, 2))
            shift_block(v, tiles - 1, 8, rows, (-2, -1))
    for n in range(tiles, tiles + 3):
        loads[n].wait()
    lax.fori_loop(1, tiles - 1, advect_inner, 0)

    def spread(piece, v):
        return pltpu.roll(piece, LANES - 2 - 2 * v, 1)

    def spread_east(piece, v):
        return pltpu.roll(piece, LANES - 2 * v, 1) if v else piece

    def rim(row0, size, from_west, from_east):
        for v in range(levels):
            ext[v, 0, row0 : row0 + size, :] = spread(from_west, v)
            ext[v, tiles + 1, row0 : row0 + size, :] = spread_east(from_east, v)

    def fill_rows(which, row0):
        for v in range(levels):
            for t in range(tiles):
                cols = slice(t * LANES, (t + 1) * LANES)
                ext[v, t + 1, row0 : row0 + 2, :] = got_row[which, 2 * v : 2 * v + 2, cols]

    @pl.when(has_up)
    def _():
        for copy in below:
            copy.wait_recv()
        fill_rows(0, 6)
        rim(0, 8, got_corner[0], got_corner[1])

    @pl.when(jnp.logical_not(has_up))
    def _():
        ext[:, :, 0:8, :] = jnp.zeros((levels, tiles + 2, 8, LANES), F32)

    @pl.when(has_down)
    def _():
        for copy in above:
            copy.wait_recv()
        fill_rows(1, rows + 8)
        rim(rows + 8, 8, got_corner[2], got_corner[3])

    @pl.when(jnp.logical_not(has_down))
    def _():
        ext[:, :, rows + 8 : rows + 16, :] = jnp.zeros((levels, tiles + 2, 8, LANES), F32)

    for copy in flat:
        copy.wait_recv()
    rim(8, rows, got_col[0], got_col[1])

    def shift_rims(t, carry):
        for v in range(levels):
            shift_block(v, t, 0, 8)
            shift_block(v, t, rows + 8, 8)
        return carry

    edges = min(tiles, 2)
    for v in range(levels):
        shift_block(v, 0, 8, rows, (-2, -1))
        shift_block(v, tiles - 1, 8, rows, (1, 2))
    lax.fori_loop(0, tiles, shift_rims, 0)
    outer = sorted({0, groups - 1})

    def advect_rims(t, carry):
        advect(t, outer)
        return carry

    def advect_edge(n, carry):
        advect(n * (tiles - 1), range(groups))
        return carry

    lax.fori_loop(0, edges, advect_edge, 0)
    lax.fori_loop(1, tiles - 1, advect_rims, 0)

    loads[tiles + 3].wait()
    contract_last = (((1,), (1,)), ((), ()))
    send_f[...] = jnp.zeros_like(send_f)
    for v in range(levels):
        value = adv[v * rows : (v + 1) * rows, :]
        lead = value.astype(BF16)
        rest = (value - lead.astype(F32)).astype(BF16)
        both = lax.dot_general(tab[...], lead, contract_last, preferred_element_type=F32)
        more = lax.dot_general(
            tab[0 : 2 * waves, :], rest, contract_last, preferred_element_type=F32
        )
        coeffs = both[0 : 2 * waves] + both[2 * waves :] + more
        send_f[v, :, 0:rows] = coeffs[0:waves]
        send_f[v, :, HALF : HALF + rows] = coeffs[waves:]
    copies_f = []
    for d in others(e, n_lev):
        copy = remote(send_f.at[d], got_f.at[e], f_send.at[d], f_recv.at[e], l, d)
        copy.start()
        copies_f.append(copy)
    got_f[e] = send_f[e]
    for d in others(e, n_lev):
        remote(send_f.at[d], got_f.at[d], f_send.at[d], f_recv.at[d], l, d).wait_recv()
    total = got_f[0]
    for d in range(1, n_lev):
        total = total + got_f[d]
    fourier = total.astype(BF16)
    send_x[...] = fourier
    copy_x = remote(send_x, got_x, x_send, x_recv, mirror, e)
    copy_x.start()

    at_row = lax.broadcasted_iota(jnp.int32, (LANES, LANES), 0)
    at_col = lax.broadcasted_iota(jnp.int32, (LANES, LANES), 1)
    flip = ((at_row + at_col == rows - 1) & (at_row < HALF) & (at_col < HALF)) | (
        (at_row + at_col == 2 * HALF + rows - 1) & (at_row >= HALF) & (at_col >= HALF)
    )
    flip = flip.astype(F32)
    sign = jnp.where(l < n_lat // 2, 1.0, -1.0).astype(F32)
    loads[tiles + 4].wait()
    copy_x.wait_recv()
    partner = jnp.dot(got_x[...], flip.astype(BF16), preferred_element_type=F32)
    combined = partner + sign * fourier.astype(F32)

    forward_scale = 1.0 / math.sqrt(rows * n_lat // 2)
    group = 16
    for k0 in range(0, waves, group):
        ks = slice(k0, k0 + group)
        real = jnp.zeros((group, steps), F32)
        imag = jnp.zeros((group, steps), F32)
        for i in range(rows):
            values = leg[i, ks, :].astype(F32)
            real = real + values * combined[ks, i : i + 1]
            imag = imag + values * combined[ks, HALF + i : HALF + i + 1]
        sums[0, ks, :] = real * forward_scale
        sums[1, ks, :] = imag * forward_scale
    for s in range(waves):
        k = inv[s]
        chg_slot[s, 0:1, :] = sums[0, pl.ds(k, 1), :]
        chg_slot[s, 1:2, :] = sums[1, pl.ds(k, 1), :]
    send_s[...] = chg_slot[...]
    own = waves // n_lat
    copies_s = []
    for d in others(l, n_lat):
        copy = remote(
            send_s.at[pl.ds(d * own, own)], got_s.at[l], s_send.at[d], s_recv.at[l], d, e
        )
        copy.start()
        copies_s.append(copy)
    got_s[l] = send_s[pl.ds(l * own, own)]
    for d in others(l, n_lat):
        remote(
            send_s.at[pl.ds(d * own, own)], got_s.at[d], s_send.at[d], s_recv.at[d], d, e
        ).wait_recv()

    column = lax.broadcasted_iota(jnp.int32, (2, steps), 1)
    for p in range(2):
        start = p * (n_lat // 2)
        raw = got_s[start]
        for d in range(start + 1, start + n_lat // 2):
            raw = raw + got_s[d]
        for so in range(own):
            wave = inv[l * own + so] * (NT + 1) // waves
            degree = wave + 2 * column + p
            factor = 1.0 / (
                1.0 + DAMPING * (degree * (degree + 1)).astype(F32) / float(NT * (NT + 1))
            )
            masked = jnp.where(degree <= NT, raw[so], 0.0)
            damped = masked * factor
            spec_ref[so, p, 0] = damped
            send_c[p, so] = (damped - masked).astype(BF16)
    copies_c = []
    parity_of = lambda d: d // (n_lat // 2)
    for d in others(l, n_lat):
        copy = remote(send_c.at[parity_of(d)], got_c.at[l], c_send.at[d], c_recv.at[l], d, e)
        copy.start()
        copies_c.append(copy)
    got_c[l] = send_c[parity_of(l)]
    for d in others(l, n_lat):
        remote(
            send_c.at[parity_of(d)], got_c.at[d], c_send.at[d], c_recv.at[d], d, e
        ).wait_recv()

    for d in range(n_lat):
        for so in range(own):
            chg_slot[d * own + so] = got_c[d, so].astype(F32)
    for k in range(waves):
        value = chg_slot[slot_ref[k]]
        chg[0, k : k + 1, :] = value[0:1]
        chg[1, k : k + 1, :] = value[1:2]
    inverse_scale = math.sqrt(NLON) / math.sqrt(waves) / math.sqrt(steps)
    lane = lax.broadcasted_iota(jnp.int32, (group, LANES), 1)
    wave_row = lax.broadcasted_iota(jnp.int32, (group, LANES), 0)
    for k0 in range(0, waves, group):
        ks = slice(k0, k0 + group)
        real, imag = chg[0, ks, :], chg[1, ks, :]
        half = jnp.zeros((group, LANES), F32)
        for i in range(rows):
            values = leg[i, ks, :].astype(F32)
            half = jnp.where(lane == i, jnp.sum(values * real, axis=1, keepdims=True), half)
            half = jnp.where(
                lane == HALF + i, jnp.sum(values * imag, axis=1, keepdims=True), half
            )
        half = half * jnp.where(wave_row + k0 == 0, inverse_scale, 2.0 * inverse_scale)
        send_h[0, ks, :] = half
        send_h[1, ks, :] = jnp.dot(
            half, flip, precision=lax.Precision.HIGHEST, preferred_element_type=F32
        )
    copies_h = []
    for off in range(n_lev):
        d = lax.rem(e + off, n_lev)
        copy = remote(send_h.at[1], got_h.at[1, e], h_send.at[1, d], h_recv.at[1, e], mirror, d)
        copy.start()
        copies_h.append(copy)
    for d in others(e, n_lev):
        copy = remote(send_h.at[0], got_h.at[0, e], h_send.at[0, d], h_recv.at[0, e], l, d)
        copy.start()
        copies_h.append(copy)
    got_h[0, e] = send_h[0]
    for d in others(e, n_lev):
        remote(
            send_h.at[0], got_h.at[0, d], h_send.at[0, d], h_recv.at[0, d], l, d
        ).wait_recv()
    for off in range(n_lev):
        d = lax.rem(e + off, n_lev)
        remote(
            send_h.at[1], got_h.at[1, d], h_send.at[1, d], h_recv.at[1, d], mirror, d
        ).wait_recv()

    stack = []
    for v in range(levels):
        synthesis = got_h[1, v] + sign * got_h[0, v]
        both = jnp.concatenate([synthesis, pltpu.roll(synthesis, HALF, 1)], axis=0)
        stack.append(jnp.transpose(both)[0:rows, :])
    synthesis = jnp.concatenate(stack, axis=0)
    lead = synthesis.astype(BF16)
    rest = (synthesis - lead.astype(F32)).astype(BF16)
    chunk = min(width, 256)
    for j in range(0, width, chunk):
        cols = slice(j, j + chunk)
        table, table_rest = tab[0 : 2 * waves, cols], tab[2 * waves :, cols]
        increment = (
            jnp.dot(lead, table, preferred_element_type=F32)
            + jnp.dot(lead, table_rest, preferred_element_type=F32)
            + jnp.dot(rest, table, preferred_element_type=F32)
        )
        updated = adv[:, cols] + increment
        for v in range(levels):
            out_ref[v, :, cols] = updated[v * rows : (v + 1) * rows]

    for copy in flat + copies_f + [copy_x] + copies_s + copies_c + copies_h:
        copy.wait_send()

    @pl.when(has_down)
    def _():
        for copy in below:
            copy.wait_send()

    @pl.when(has_up)
    def _():
        for copy in above:
            copy.wait_send()


def solution(mesh):
    n_lat, n_lev = mesh.shape["lat"], mesh.shape["lev"]

    def on_device(field, weights, depart_row, depart_col, legendre, wave_slot):
        levels, rows, width = field.shape
        _, waves, steps = legendre.shape
        tiles = width // LANES
        own = waves // n_lat
        table = jnp.asarray(lon_table(waves))
        vmem, dma = pltpu.VMEM, pltpu.SemaphoreType.DMA
        anywhere = pl.BlockSpec(memory_space=pltpu.HBM)
        in_vmem = pl.BlockSpec(memory_space=pltpu.VMEM)
        return pl.pallas_call(
            functools.partial(kernel, n_lat, n_lev),
            out_shape=(
                jax.ShapeDtypeStruct((levels, rows, width), F32),
                jax.ShapeDtypeStruct((own, 2, 1, 2, steps), F32),
            ),
            in_specs=[pl.BlockSpec(memory_space=pltpu.SMEM)] + [anywhere] * 6,
            out_specs=(in_vmem, in_vmem),
            scratch_shapes=[
                vmem((levels, tiles + 2, rows + 16, LANES), F32),
                vmem((4, levels, tiles, rows + 16, LANES), F32),
                vmem((4, rows, width), BF16),
                vmem((rows, width), jnp.int32),
                vmem((rows, width), jnp.int32),
                vmem((rows, waves, steps), BF16),
                vmem((4 * waves, width), BF16),
                vmem((levels * rows, width), F32),
                pltpu.SMEM((waves,), jnp.int32),
                vmem((2, 2 * levels, width), F32),
                vmem((2, rows, LANES), F32),
                vmem((2, 2 * levels, width), F32),
                vmem((2, rows, LANES), F32),
                vmem((4, 8, LANES), F32),
                vmem((n_lev, waves, LANES), F32),
                vmem((n_lev, waves, LANES), F32),
                vmem((waves, LANES), BF16),
                vmem((waves, LANES), BF16),
                vmem((2, waves, steps), F32),
                vmem((waves, 2, steps), F32),
                vmem((n_lat, own, 2, steps), F32),
                vmem((2, own, 2, steps), BF16),
                vmem((n_lat, own, 2, steps), BF16),
                vmem((waves, 2, steps), F32),
                vmem((2, waves, steps), F32),
                vmem((2, waves, LANES), F32),
                vmem((2, n_lev, waves, LANES), F32),
                dma((tiles + 5,)),
                dma((8,)), dma((8,)),
                dma((n_lev,)), dma((n_lev,)),
                dma, dma,
                dma((n_lat,)), dma((n_lat,)),
                dma((n_lat,)), dma((n_lat,)),
                dma((2, n_lev)), dma((2, n_lev)),
            ],
            compiler_params=pltpu.CompilerParams(
                collective_id=0, has_side_effects=True, vmem_limit_bytes=63 << 20
            ),
        )(wave_slot, field, weights, depart_row, depart_col, legendre, table)

    placed = (
        P(None, "lat", "lev"),
        P(None, "lat", "lev"),
        P("lat", "lev"),
        P("lat", "lev"),
        P("lat", None, None),
        P(),
    )
    return jax.shard_map(
        on_device,
        mesh=mesh,
        in_specs=placed,
        out_specs=(P(None, "lat", "lev"), P("lat", None, "lev", None, None)),
        check_vma=False,
    )
```
